32 devices in a mesh: ctx: 16 (over z, y, x), fsdp: 2 (over core).
Axes of the slice: x: 2, y: 2, z: 4, core: 2. Of those that a mesh axis runs over, the one named last changes fastest.
Arguments:
- inputs: bfloat16 [2, 2048, 1024], P('fsdp', 'ctx'), may hold values from -48 to 48
- cotangent: bfloat16 [2, 2048, 1024], P('fsdp', 'ctx'), may hold values from -6 to 6
- doc_lengths: int32 [2, 8], P('fsdp'), may hold values from 1 to 1024, 2048 in all within a row
- qkv_weight: bfloat16 [1024, 3072], P('fsdp'), may hold values from -0.1875 to 0.1875
- out_weight: bfloat16 [1024, 1024], P('fsdp'), may hold values from -0.1875 to 0.1875
- fc1_weight: bfloat16 [1024, 4096], P('fsdp'), may hold values from -0.1875 to 0.1875
- fc2_weight: bfloat16 [4096, 1024], P('fsdp'), may hold values from -0.09375 to 0.09375
- norm_gain: bfloat16 [3, 1024], P(None, 'fsdp'), may hold values from 0.099609375 to 1.8984375
- norm_bias: bfloat16 [3, 1024], P(None, 'fsdp'), may hold values from -1.5 to 1.5
- mid_gain: bfloat16 [4096], P('fsdp'), may hold values from 0.099609375 to 1.8984375
- mid_bias: bfloat16 [4096], P('fsdp'), may hold values from -1.5 to 1.5
- head_scale: bfloat16 [16], P('fsdp'), may hold values from 0.5 to 2
Outputs:
- output: bfloat16 [2, 2048, 1024], P('fsdp', 'ctx')
- input_grad: bfloat16 [2, 2048, 1024], P('fsdp', 'ctx')
- qkv_grad: float32 [1024, 3072], P('fsdp')
- out_grad: float32 [1024, 1024], P('fsdp')
- fc1_grad: float32 [1024, 4096], P('fsdp')
- fc2_grad: float32 [4096, 1024], P('fsdp')
- gain_grad: float32 [3, 1024], P(None, 'fsdp')
- bias_grad: float32 [3, 1024], P(None, 'fsdp')
- mid_gain_grad: float32 [4096], P('fsdp')
- mid_bias_grad: float32 [4096], P('fsdp')
- scale_grad: float32 [16], P('fsdp')
- rms_values: float32 [3], replicated
The draws below stay inside these ranges and needn't reach their ends.
Inputs may be any that keep to these rules, and one draw needn't show every extreme that they name: `doc_lengths`: each row holds 8 document lengths that sum to 2048; the longest is 1024.
All inputs are finite; a program needn't handle non-finite values.
Results may differ from the reference program's by a relative error of at most 0.022.
Values may be sent and summed in bfloat16 or wider, within the bound.
No kernel may reach another device: no remote copies, remote signals or barrier semaphores. Data moves between devices by JAX's collectives and lax.ppermute only.
A program may use at most 320 MiB of HBM per device.

```python
import math
import jax
import jax.numpy as jnp
import numpy as np
from jax import lax

D = 1024
HEADS = 16
HEAD_DIM = 64
FF = 4096
NDOC = 8
HALF = 64
STREAM = 2048
STREAMS = 2
MAXDOC = 1024
N_CTX = 16


def draw_inputs(key, part):
    key_base, key_row, key_run = jax.random.split(key, 3)
    full_shape = (STREAMS, STREAM, D)
    row_scale = jnp.exp(jax.random.uniform(key_row, (STREAMS, STREAM, 1), jnp.float32, -0.35, 0.35))
    run_scale = jnp.repeat(jnp.exp(jax.random.uniform(key_run, (STREAMS, STREAM // HALF, 1), jnp.float32, -0.35, 0.35)), HALF, axis=1)
    row_place = jnp.arange(STREAM, dtype=jnp.float32).reshape(1, STREAM, 1) / max(STREAM - 1, 1)
    rising = jnp.exp(math.log(3.0) * row_place)
    base = jnp.clip(jax.random.normal(key_base, full_shape, jnp.float32), -4.0, 4.0)
    return (base * row_scale * run_scale * rising).astype(jnp.bfloat16)


def block_scale(rng, dims, cuts, low, largest):
    def one(position, shards_of):
        steps = jax.random.uniform(jax.random.fold_in(jax.random.fold_in(rng, 6), position), (shards_of,), jnp.float32, low / len(cuts), largest / len(cuts))
        return jnp.repeat(jnp.exp(steps), dims[position] // shards_of).reshape((-1,) + (1,) * (len(dims) - position - 1))

    loudness = one(*cuts[0])
    for cut in cuts[1:]:
        loudness = loudness * one(*cut)
    return loudness


def split_up(amount, total, limit, skew):
    portions = [(1 << 20) // math.isqrt(grade ** skew) + 1 for grade in range(2, amount + 1)]
    rest, given = total - limit - (amount - 1), [1] * (amount - 1)
    while rest > 0:
        movable = [i for i in range(amount - 1) if given[i] < limit]
        mass, budget = sum([portions[i] for i in movable]), rest
        for i in movable:
            addition = min(limit - given[i], max(1, budget * portions[i] // mass), rest)
            given[i] = given[i] + addition
            rest = rest - addition
    return np.array([limit] + given)


def ragged(own_key, amount, total, limit, slope):
    if amount == 2:
        one = jax.random.randint(own_key, (), max(1, total - limit), min(limit, total - 1) + 1)
        return jnp.stack([one, total - one])
    sizes = jnp.asarray(split_up(amount, total, limit, slope), jnp.int32)
    twos = (amount - 1) // 2
    source_of, receiver = sizes[1:1 + 2 * twos:2], sizes[2:2 + 2 * twos:2]
    slack = jnp.minimum(source_of - 1, limit - receiver)
    moved = jax.random.randint(jax.random.fold_in(own_key, 1), (twos,), 0, 1 << 20) % (slack + 1)
    sizes = sizes.at[1:1 + 2 * twos:2].set(source_of - moved).at[2:2 + 2 * twos:2].set(receiver + moved)
    return sizes[jax.random.permutation(jax.random.fold_in(own_key, 2), amount)]


def bell_draw(key, shape, scale, limit, cuts=(), held_as=jnp.bfloat16):
    drawn = jax.random.normal(key, shape, jnp.float32) * scale
    if len(cuts) > 0:
        drawn = block_scale(key, shape, cuts, -0.22, 0.18) * drawn
    return jnp.clip(drawn, min=-limit, max=limit).astype(held_as)


def setup_inputs(seed: int = 0) -> dict:
    seeds = jax.random.split(jax.random.key(seed), 13)
    return {
        "inputs": draw_inputs(jax.random.fold_in(seeds[12], 71), 0),
        "cotangent": bell_draw(seeds[1], (STREAMS, STREAM, D), 1.0, 6.0, ((0, 2), (1, 16))),
        "doc_lengths": jax.vmap(lambda own: ragged(own, NDOC, STREAM, MAXDOC, 2))(jax.random.split(seeds[2], STREAMS)).reshape((STREAMS, NDOC)).astype(jnp.int32),
        "qkv_weight": bell_draw(seeds[3], (D, 3 * D), D ** -0.5, 0.1875, ((0, 2),)),
        "out_weight": bell_draw(seeds[4], (D, D), D ** -0.5, 0.1875, ((0, 2),)),
        "fc1_weight": bell_draw(seeds[5], (D, FF), D ** -0.5, 0.1875, ((0, 2),)),
        "fc2_weight": bell_draw(seeds[6], (FF, D), FF ** -0.5, 0.09375, ((0, 2),)),
        "norm_gain": jnp.clip(1.0 + 0.18 * jax.random.normal(seeds[7], (3, D), jnp.float32), 0.099609375, 1.8984375).astype(jnp.bfloat16),
        "norm_bias": bell_draw(seeds[8], (3, D), 0.3, 1.5, ((1, 2),)),
        "mid_gain": jnp.clip(1.0 + 0.18 * jax.random.normal(seeds[9], (FF,), jnp.float32), 0.099609375, 1.8984375).astype(jnp.bfloat16),
        "mid_bias": bell_draw(seeds[10], (FF,), 0.3, 1.5, ((0, 2),)),
        "head_scale": jnp.clip(jnp.exp(math.log(2.0) - 1.3862944 * jax.random.uniform(seeds[11], (HEADS,), jnp.float32) ** block_scale(seeds[11], (HEADS,), ((0, 2),), -0.2, 0.2)), 0.5, 2.0).astype(jnp.bfloat16),
    }


@jax.custom_vjp
def low(v):
    return lax.optimization_barrier(v.astype(jnp.bfloat16)).astype(jnp.float32)

@jax.custom_vjp
def low_back(v):
    return v

def low_keep(v):
    return (low(v), None)

def low_pass(kept, grad):
    return (grad,)

def back_keep(v):
    return (v, None)

def back_low(kept, grad):
    return (low(grad),)
low.defvjp(low_keep, low_pass)
low_back.defvjp(back_keep, back_low)
epsilon = 1e-05

def stored_positions(first_row, n_rows, half_rows, groups):
    offsets = first_row + jnp.arange(n_rows, dtype=jnp.int32)
    halves = offsets // half_rows
    paired = halves // 2
    placed = jnp.where(halves % 2 == 0, paired, 2 * groups - 1 - paired)
    return (placed * half_rows + offsets % half_rows).astype(jnp.int32)

def doc_floor(positions, starts):
    begun_mask = starts[None, :] <= positions[:, None]
    return lax.optimization_barrier(jnp.max(jnp.where(begun_mask, starts[None, :], 0), axis=1)).astype(jnp.int32)

def layer_norm(values, gain_vec, bias_vec):
    centered = values - lax.optimization_barrier(jnp.mean(values, axis=-1, keepdims=True))
    inverse = lax.rsqrt(lax.optimization_barrier(jnp.mean(centered * centered, axis=-1, keepdims=True)) + epsilon)
    return centered * inverse * gain_vec + bias_vec

def matmul(left, right):
    return jnp.dot(left, right, precision=lax.Precision.HIGHEST)

def forward(inputs, qkv_weight, out_weight, fc1_weight, fc2_weight, norm_gain, norm_bias, mid_gain, mid_bias, head_scale, positions, floors):
    length = inputs.shape[0]
    normed_one = low(layer_norm(inputs, norm_gain[0], norm_bias[0]))
    project = matmul(normed_one, qkv_weight)
    queries = low_back(low(project[:, :D])).reshape(length, HEADS, HEAD_DIM)
    key_heads = low_back(low(project[:, D:2 * D])).reshape(length, HEADS, HEAD_DIM)
    value_heads = low_back(low(project[:, 2 * D:])).reshape(length, HEADS, HEAD_DIM)
    block_rows = math.gcd(length, 512)

    def attend(block_first):
        query_blk = lax.dynamic_slice_in_dim(queries, block_first, block_rows, 0)
        query_pos = lax.dynamic_slice_in_dim(positions, block_first, block_rows, 0)
        query_floor = lax.dynamic_slice_in_dim(floors, block_first, block_rows, 0)
        scores = low_back(jnp.einsum('qhe,khe->qhk', query_blk, key_heads, precision=lax.Precision.HIGHEST) * HEAD_DIM ** (-0.5))
        allowed = (positions[None, :] <= query_pos[:, None]) & (positions[None, :] >= query_floor[:, None])
        masked = jnp.where(allowed[:, None, :], scores, -1e+30)
        shifted = jnp.exp(masked - lax.optimization_barrier(jnp.max(masked, axis=-1, keepdims=True)))
        weights = low(shifted / lax.optimization_barrier(jnp.sum(shifted, axis=-1, keepdims=True)))
        return low_back(jnp.einsum('qhk,khe->qhe', weights, value_heads, precision=lax.Precision.HIGHEST))
    firsts = (block_rows * jnp.arange(length // block_rows)).astype(jnp.int32)
    attended = lax.map(jax.checkpoint(attend), firsts).reshape(length, HEADS, HEAD_DIM)
    scaled = low((attended * head_scale[None, :, None]).reshape(length, D))
    branch = low_back(matmul(scaled, out_weight))
    attn_out = layer_norm(branch, norm_gain[1], norm_bias[1])
    middle = inputs + attn_out
    normed_two = low(layer_norm(middle, norm_gain[2], norm_bias[2]))
    hidden = low_back(matmul(normed_two, fc1_weight))
    mixed_in = low(layer_norm(jax.nn.gelu(hidden, approximate=True), mid_gain, mid_bias))
    ffn_out = low_back(matmul(mixed_in, fc2_weight))
    return (middle + ffn_out, (attn_out, ffn_out))

def reference(inputs, cotangent, doc_lengths, qkv_weight, out_weight, fc1_weight, fc2_weight, norm_gain, norm_bias, mid_gain, mid_bias, head_scale):
    params = tuple((item.astype(jnp.float32) for item in (qkv_weight, out_weight, fc1_weight, fc2_weight, norm_gain, norm_bias, mid_gain, mid_bias, head_scale)))
    positions = stored_positions(0, STREAM, HALF, N_CTX)

    def one_stream(totals, scanned):
        stream_in, stream_cot, lengths_row = scanned
        starts = (jnp.cumsum(lengths_row) - lengths_row).astype(jnp.int32)
        floors = doc_floor(positions, starts)

        def wrapped(stream_x, *weights):
            return forward(stream_x, *weights, positions, floors)
        result, pullback, branches = jax.vjp(wrapped, stream_in.astype(jnp.float32), *params, has_aux=True)
        gradients = pullback(stream_cot.astype(jnp.float32))
        attn_out, ffn_out = branches
        squares = jnp.stack([jnp.sum(result * result), jnp.sum(attn_out * attn_out), jnp.sum(ffn_out * ffn_out)])
        summed = tuple((before + added for before, added in zip(totals[0], gradients[1:])))
        return ((summed, totals[1] + squares), (result.astype(jnp.bfloat16), gradients[0].astype(jnp.bfloat16)))
    start_totals = (tuple((jnp.zeros_like(item) for item in params)), jnp.zeros((3,), jnp.float32))
    final_totals, stacked = lax.scan(one_stream, start_totals, (inputs, cotangent, doc_lengths))
    grads_all, squares_all = final_totals
    rms_values = jnp.sqrt(squares_all / (STREAMS * STREAM * D))
    return (stacked[0], stacked[1], grads_all[0], grads_all[1], grads_all[2], grads_all[3], grads_all[4], grads_all[5], grads_all[6], grads_all[7], grads_all[8], rms_values)
```

```python
from functools import partial

import jax
import jax.numpy as jnp
from jax import lax
from jax.experimental import pallas as pl
from jax.experimental.pallas import tpu as pltpu
from jax.sharding import PartitionSpec as P

HEADS = 16
HEAD_DIM = 64
TILE = 256
EPS = 1e-05
MASKED = -1e30
SCALE = HEAD_DIM ** (-0.5)


def dot(a, b, ca=1, cb=0):
    return lax.dot_general(a, b, (((ca,), (cb,)), ((), ())), preferred_element_type=jnp.float32)


def normalize(values):
    centered = values - jnp.mean(values, axis=-1, keepdims=True)
    inverse = lax.rsqrt(jnp.mean(centered * centered, axis=-1, keepdims=True) + EPS)
    return (centered * inverse, inverse)


def norm_backward(grad_out, normed, inverse, gain_vec):
    grad_normed = grad_out * gain_vec
    grad_in = inverse * (
        grad_normed
        - jnp.mean(grad_normed, axis=-1, keepdims=True)
        - normed * jnp.mean(grad_normed * normed, axis=-1, keepdims=True)
    )
    return (grad_in, jnp.sum(grad_out * normed, axis=0), jnp.sum(grad_out, axis=0))


def sorted_sources(n_tiles):
    return [(t, 0) for t in range(n_tiles)] + [(t, 1) for t in range(n_tiles - 1, -1, -1)]


def pair_up(first, second):
    lane = lax.broadcasted_iota(jnp.int32, first[0].shape, 1)
    left = first[0] if first[1] == 0 else pltpu.roll(first[0], 64, 1)
    right = second[0] if second[1] == 1 else pltpu.roll(second[0], 64, 1)
    return jnp.where(lane < 64, left, right)


def sort_tiles(load, n_tiles, store):
    order = sorted_sources(n_tiles)
    for u in range(n_tiles):
        (ta, ha), (tb, hb) = order[2 * u], order[2 * u + 1]
        store(u, pair_up((load(ta), ha), (load(tb), hb)))


def unsort_tiles(load, n_tiles, store):
    for t in range(n_tiles):
        a, b = t, 2 * n_tiles - 1 - t
        store(t, pair_up((load(a // 2), a % 2), (load(b // 2), b % 2)))


def tile_spans(info_ref, qt, n_q_tiles, half_run, total_blocks):
    group = info_ref[0]
    per_run = n_q_tiles // 2
    low_first = group * half_run
    high_first = total_blocks * 64 - (group + 1) * half_run
    q_first = jnp.where(qt < per_run, low_first + qt * TILE, high_first + (qt - per_run) * TILE)
    start = jnp.int32(0)
    floor_first = jnp.int32(0)
    for d in range(8):
        floor_first = jnp.where(start <= q_first, start, floor_first)
        start = start + info_ref[1 + d]
    return q_first, floor_first // TILE


def query_rows(info_ref, q_first):
    q_pos = q_first + lax.broadcasted_iota(jnp.int32, (1, TILE), 1)
    start = jnp.int32(0)
    floor = jnp.zeros((1, TILE), jnp.int32)
    for d in range(8):
        floor = jnp.where(q_pos >= start, start, floor)
        start = start + info_ref[1 + d]
    return q_pos, floor


def usable_mask(q_pos, floor, kt):
    k_pos = kt * TILE + lax.broadcasted_iota(jnp.int32, (TILE, TILE), 0)
    return (k_pos <= q_pos) & (k_pos >= floor)


def attend_kernel(
    info_ref, hs_ref, q_ref, kv_ref, scaled_ref, att_ref, log_ref, qs_ref, ks_ref, vs_ref, kn_ref,
    *, n_q, n_k, k_at,
):
    per = TILE // 128
    f32 = jnp.float32

    def put(ref):
        def store(u, tile):
            ref[u // per, :, (u % per) * 128 : (u % per) * 128 + 128] = tile.astype(jnp.bfloat16)
        return store

    sort_tiles(lambda t: q_ref[t, 0].astype(f32), n_q, put(qs_ref))
    sort_tiles(lambda t: kv_ref[t, k_at].astype(f32), n_k, put(ks_ref))
    sort_tiles(lambda t: kv_ref[t, k_at + 1].astype(f32), n_k, put(vs_ref))
    for kt in range(n_k // per):
        kn_ref[kt] = ks_ref[kt].astype(f32).T.astype(jnp.bfloat16)

    def one_query_tile(qt, carry):
        q_first, k_low = tile_spans(info_ref, qt, n_q // per, n_q * 64, 2 * n_k)
        q_pos, floor = query_rows(info_ref, q_first)
        q_t = qs_ref[qt]

        def one_key_tile(kt, state):
            high, total, acc = state
            scores = dot(kn_ref[kt], q_t) * SCALE
            usable = usable_mask(q_pos, floor, kt)
            scores = jnp.where(usable, scores, MASKED)
            new_high = jnp.maximum(high, jnp.max(scores, axis=0, keepdims=True))
            probs = jnp.where(usable, jnp.exp(scores - new_high), 0.0)
            fix = jnp.exp(high - new_high)
            total = total * fix + jnp.sum(probs, axis=0, keepdims=True)
            acc = acc * fix + dot(vs_ref[kt], probs.astype(jnp.bfloat16))
            return new_high, total, acc

        high, total, acc = lax.fori_loop(
            k_low,
            q_first // TILE + 1,
            one_key_tile,
            (
                jnp.full((1, TILE), MASKED, f32),
                jnp.zeros((1, TILE), f32),
                jnp.zeros((HEAD_DIM, TILE), f32),
            ),
        )
        att_ref[qt] = acc / total
        log_ref[qt] = high + jnp.log(total)
        return carry

    lax.fori_loop(0, n_q // per, one_query_tile, 0)
    head_scale = hs_ref[0]

    def load(u):
        return att_ref[u // per, :, (u % per) * 128 : (u % per) * 128 + 128]

    def give(t, tile):
        scaled_ref[t] = (tile * head_scale).astype(jnp.bfloat16)

    unsort_tiles(load, n_q, give)


def attend_back_kernel(
    info_ref, qs_ref, ks_ref, vs_ref, att_ref, log_ref, go_ref, dq_ref, dk_ref, dv_ref, dsum_ref,
    go_s, kn_ref, vn_ref, dq_s, dk_s, dv_s,
    *, n_q, n_k,
):
    per = TILE // 128
    f32 = jnp.float32
    low = jnp.bfloat16

    def store(u, tile):
        go_s[u // per, :, (u % per) * 128 : (u % per) * 128 + 128] = tile.astype(low)

    sort_tiles(lambda t: go_ref[t].astype(f32), n_q, store)
    for kt in range(n_k // per):
        kn_ref[kt] = ks_ref[kt].astype(f32).T.astype(low)
        vn_ref[kt] = vs_ref[kt].astype(f32).T.astype(low)
        dk_s[kt] = jnp.zeros((TILE, HEAD_DIM), f32)
        dv_s[kt] = jnp.zeros((TILE, HEAD_DIM), f32)
    dsum_ref[...] = jnp.zeros((1, TILE), f32)

    def one_query_tile(qt, carry):
        q_first, k_low = tile_spans(info_ref, qt, n_q // per, n_q * 64, 2 * n_k)
        q_pos, floor = query_rows(info_ref, q_first)
        q_t = qs_ref[qt]
        g_t = go_s[qt]
        q_n = q_t.astype(f32).T.astype(low)
        g_n = g_t.astype(f32).T.astype(low)
        log_total = log_ref[qt]
        delta = jnp.sum(g_t.astype(f32) * att_ref[qt], axis=0, keepdims=True)
        dsum_ref[...] += delta

        def one_key_tile(kt, acc):
            scores = dot(kn_ref[kt], q_t) * SCALE
            usable = usable_mask(q_pos, floor, kt)
            probs = jnp.where(usable, jnp.exp(scores - log_total), 0.0)
            grad_probs = dot(vn_ref[kt], g_t)
            grad_scores = (probs * (grad_probs - delta)).astype(low)
            dv_s[kt] += dot(probs.astype(low), g_n)
            dk_s[kt] += dot(grad_scores, q_n)
            return acc + dot(ks_ref[kt], grad_scores)

        dq_s[qt] = lax.fori_loop(
            k_low, q_first // TILE + 1, one_key_tile, jnp.zeros((HEAD_DIM, TILE), f32)
        )
        return carry

    lax.fori_loop(0, n_q // per, one_query_tile, 0)

    def load_q(u):
        return dq_s[u // per, :, (u % per) * 128 : (u % per) * 128 + 128]

    def give_q(t, tile):
        dq_ref[t] = (tile * SCALE).astype(dq_ref.dtype)

    def load_k(u):
        return dk_s[u // per, (u % per) * 128 : (u % per) * 128 + 128, :].T

    def give_k(t, tile):
        dk_ref[t] = (tile * SCALE).astype(dk_ref.dtype)

    def load_v(u):
        return dv_s[u // per, (u % per) * 128 : (u % per) * 128 + 128, :].T

    def give_v(t, tile):
        dv_ref[t] = tile.astype(dv_ref.dtype)

    unsort_tiles(load_q, n_q, give_q)
    unsort_tiles(load_k, n_k, give_k)
    unsort_tiles(load_v, n_k, give_v)


def on_chip(n):
    return [pl.BlockSpec(memory_space=pltpu.VMEM)] * n


def in_scalars(n):
    return [pl.BlockSpec(memory_space=pltpu.SMEM)] * n


def attend(info, head_scale, q_tiles, kv_tiles, k_at):
    n_q, n_k = q_tiles.shape[0], kv_tiles.shape[0]
    nq, nk = n_q * 128 // TILE, n_k * 128 // TILE
    low, f32 = jnp.bfloat16, jnp.float32
    return pl.pallas_call(
        partial(attend_kernel, n_q=n_q, n_k=n_k, k_at=k_at),
        in_specs=in_scalars(2) + on_chip(2),
        out_specs=tuple(on_chip(6)),
        out_shape=(
            jax.ShapeDtypeStruct((n_q, HEAD_DIM, 128), low),
            jax.ShapeDtypeStruct((nq, HEAD_DIM, TILE), f32),
            jax.ShapeDtypeStruct((nq, 1, TILE), f32),
            jax.ShapeDtypeStruct((nq, HEAD_DIM, TILE), low),
            jax.ShapeDtypeStruct((nk, HEAD_DIM, TILE), low),
            jax.ShapeDtypeStruct((nk, HEAD_DIM, TILE), low),
        ),
        scratch_shapes=[pltpu.VMEM((nk, TILE, HEAD_DIM), low)],
        compiler_params=pltpu.CompilerParams(vmem_limit_bytes=48 << 20),
        name="attend",
    )(info, head_scale, q_tiles, kv_tiles)


def attend_back(info, qs, ks, vs, att, log_total, grad_tiles, kv_type):
    n_q = grad_tiles.shape[0]
    nq, nk = qs.shape[0], ks.shape[0]
    n_k = nk * TILE // 128
    low, f32 = jnp.bfloat16, jnp.float32
    return pl.pallas_call(
        partial(attend_back_kernel, n_q=n_q, n_k=n_k),
        in_specs=in_scalars(1) + on_chip(6),
        out_specs=tuple(on_chip(4)),
        out_shape=(
            jax.ShapeDtypeStruct((n_q, HEAD_DIM, 128), low),
            jax.ShapeDtypeStruct((n_k, HEAD_DIM, 128), kv_type),
            jax.ShapeDtypeStruct((n_k, HEAD_DIM, 128), kv_type),
            jax.ShapeDtypeStruct((1, TILE), f32),
        ),
        scratch_shapes=[
            pltpu.VMEM((nq, HEAD_DIM, TILE), low),
            pltpu.VMEM((nk, TILE, HEAD_DIM), low),
            pltpu.VMEM((nk, TILE, HEAD_DIM), low),
            pltpu.VMEM((nq, HEAD_DIM, TILE), f32),
            pltpu.VMEM((nk, TILE, HEAD_DIM), f32),
            pltpu.VMEM((nk, TILE, HEAD_DIM), f32),
        ],
        compiler_params=pltpu.CompilerParams(vmem_limit_bytes=48 << 20),
        name="attend_back",
    )(info, qs, ks, vs, att, log_total, grad_tiles)


def from_member(value, s, size):
    return lax.ppermute(value, "fsdp", [((i + s) % size, i) for i in range(size)])


def gather_parts(shard, size):
    return [shard] + [from_member(shard, s, size) for s in range(1, size)]


def part_of(value, s, me, size, axis):
    width = value.shape[axis] // size
    return lax.dynamic_slice_in_dim(value, ((me + s) % size) * width, width, axis)


def natural(parts, me, axis):
    size = len(parts)
    twice = jnp.concatenate(parts + parts, axis=axis)
    width = parts[0].shape[axis]
    return lax.dynamic_slice_in_dim(twice, ((size - me) % size) * width, size * width, axis)


def times_parts(value, parts, me):
    size = len(parts)
    total = dot(part_of(value, 0, me, size, 1), parts[0])
    for s in range(1, size):
        total = total + dot(part_of(value, s, me, size, 1), parts[s])
    return total


def all_tokens(value, size):
    return jnp.concatenate([value] + [from_member(value, s, size) for s in range(1, size)], axis=0)


def all_tokens_own(value, me, size):
    pieces = [part_of(value, 0, me, size, 1)]
    for s in range(1, size):
        pieces.append(from_member(part_of(value, size - s, me, size, 1), s, size))
    return jnp.concatenate(pieces, axis=0)


def local(
    inputs, cotangent, doc_lengths, qkv_weight, out_weight, fc1_weight, fc2_weight,
    norm_gain, norm_bias, mid_gain, mid_bias, head_scale,
):
    low, f32 = jnp.bfloat16, jnp.float32
    groups = lax.axis_size("ctx")
    size = lax.axis_size("fsdp")
    member = lax.axis_index("ctx")
    me = lax.axis_index("fsdp")
    x_low = inputs[0]
    rows, width = x_low.shape
    hidden_width = fc1_weight.shape[1]
    copies = groups // HEADS
    head_groups = [[g * HEADS + i for i in range(HEADS)] for g in range(copies)]
    copy_groups = [[g * HEADS + i for g in range(copies)] for i in range(HEADS)]
    head = member % HEADS
    info = jnp.concatenate([(member // HEADS)[None].astype(jnp.int32), doc_lengths[0]])

    qkv_parts = gather_parts(qkv_weight, size)
    small = jnp.concatenate(
        [norm_gain.reshape(-1), norm_bias.reshape(-1), mid_gain, mid_bias, head_scale]
    )
    smalls = gather_parts(small, size)
    out_parts = gather_parts(out_weight, size)
    fc1_parts = gather_parts(fc1_weight, size)
    fc2_parts = gather_parts(fc2_weight, size)

    n_norm = norm_gain.size
    n_mid = mid_gain.size
    n_head = head_scale.size
    cut = [0, n_norm, 2 * n_norm, 2 * n_norm + n_mid, 2 * n_norm + 2 * n_mid, small.size]
    fields = [[s[cut[i] : cut[i + 1]] for s in smalls] for i in range(5)]
    gains = natural([f.reshape(3, -1) for f in fields[0]], me, 1).astype(f32)
    biases = natural([f.reshape(3, -1) for f in fields[1]], me, 1).astype(f32)
    mid_gains = natural(fields[2], me, 0).astype(f32)
    mid_biases = natural(fields[3], me, 0).astype(f32)
    head_scales = natural(fields[4], me, 0).astype(f32)
    my_scale = lax.dynamic_slice_in_dim(head_scales, head, 1, 0)

    x_local = x_low.astype(f32)
    norm_one, inv_one = normalize(x_local)
    normed_one = (norm_one * gains[0] + biases[0]).astype(low)
    project_t = sum(
        dot(qkv_parts[s], part_of(normed_one, s, me, size, 1), 0, 1) for s in range(size)
    ).astype(low)
    by_head = project_t.reshape(3, HEADS, HEAD_DIM, rows).transpose(1, 0, 2, 3)
    qkv_tiles = lax.all_to_all(by_head, "ctx", 0, 0, tiled=True, axis_index_groups=head_groups)
    if copies == 1:
        kv_tiles, k_at = qkv_tiles, 1
    else:
        kv_tiles, k_at = lax.all_gather(
            qkv_tiles[:, 1:], "ctx", axis=0, tiled=True, axis_index_groups=copy_groups
        ), 0
    scaled_tiles, att, log_total, qs, ks, vs = attend(info, my_scale, qkv_tiles, kv_tiles, k_at)
    scaled_t = lax.all_to_all(
        scaled_tiles, "ctx", 0, 0, tiled=True, axis_index_groups=head_groups
    ).reshape(width, rows)
    branch = sum(dot(part_of(scaled_t, s, me, size, 0), out_parts[s], 0, 0) for s in range(size))
    norm_att, inv_att = normalize(branch)
    attn_out = norm_att * gains[1] + biases[1]
    middle = x_local + attn_out
    norm_two, inv_two = normalize(middle)
    normed_two = (norm_two * gains[2] + biases[2]).astype(low)
    hidden = times_parts(normed_two, fc1_parts, me)
    active, gelu_back = jax.vjp(partial(jax.nn.gelu, approximate=True), hidden)
    norm_mid, inv_mid = normalize(active)
    mixed_in = (norm_mid * mid_gains + mid_biases).astype(low)
    ffn_out = times_parts(mixed_in, fc2_parts, me)
    result = middle + ffn_out

    grad_ffn = cotangent[0]
    grad_top = grad_ffn.astype(f32)
    fc2_grad = dot(all_tokens_own(mixed_in, me, size), all_tokens(grad_ffn, size), 0, 0).astype(low)
    grad_mixed = natural([dot(grad_ffn, part, 1, 1) for part in fc2_parts], me, 1)
    grad_active, mid_gain_grad, mid_bias_grad = norm_backward(
        grad_mixed, norm_mid, inv_mid, mid_gains
    )
    grad_hidden = gelu_back(grad_active)[0].astype(low)
    fc1_grad = dot(
        all_tokens_own(normed_two, me, size), all_tokens(grad_hidden, size), 0, 0
    ).astype(low)
    fc2_sum, fc1_sum = lax.psum((fc2_grad, fc1_grad), "ctx")
    grad_two = natural([dot(grad_hidden, part, 1, 1) for part in fc1_parts], me, 1)
    grad_mid_in, gain_two, bias_two = norm_backward(grad_two, norm_two, inv_two, gains[2])
    grad_middle = grad_top + grad_mid_in
    grad_branch_f, gain_att, bias_att = norm_backward(grad_middle, norm_att, inv_att, gains[1])
    grad_branch = grad_branch_f.astype(low)
    out_grad = dot(
        all_tokens_own(scaled_t.T, me, size), all_tokens(grad_branch, size), 0, 0
    ).astype(low)
    grad_scaled_t = natural([dot(part, grad_branch, 1, 1) for part in out_parts], me, 0)
    grad_att = (
        grad_scaled_t.reshape(HEADS, HEAD_DIM, rows) * head_scales[:, None, None]
    ).astype(low)
    grad_tiles = lax.all_to_all(grad_att, "ctx", 0, 0, tiled=True, axis_index_groups=head_groups)
    dq, dk, dv, delta_sum = attend_back(
        info, qs, ks, vs, att, log_total, grad_tiles, low if copies == 1 else f32
    )
    if copies > 1:
        dk, dv = (
            lax.psum_scatter(
                d, "ctx", scatter_dimension=0, tiled=True, axis_index_groups=copy_groups
            ).astype(low)
            for d in (dk, dv)
        )
    grads_out = jnp.stack([dq, dk, dv], axis=1)
    grad_proj_t = lax.all_to_all(
        grads_out, "ctx", 0, 0, tiled=True, axis_index_groups=head_groups
    ).transpose(1, 0, 2, 3).reshape(3 * width, rows)
    qkv_grad = dot(
        all_tokens_own(normed_one, me, size), all_tokens(grad_proj_t.T, size), 0, 0
    ).astype(low)
    fc2_sum, fc1_sum, out_grad, qkv_grad = lax.optimization_barrier(
        (fc2_sum, fc1_sum, out_grad, qkv_grad)
    )
    out_sum, qkv_sum = lax.psum((out_grad, qkv_grad), "ctx")
    grad_one = natural([dot(grad_proj_t, part, 0, 1) for part in qkv_parts], me, 1)
    grad_first, gain_one, bias_one = norm_backward(grad_one, norm_one, inv_one, gains[0])
    input_grad = (grad_middle + grad_first).astype(low)[None]

    my_scale_grad = jnp.sum(delta_sum) / my_scale[0]
    scale_grad = jnp.where(jnp.arange(HEADS) == head, my_scale_grad, 0.0)
    squares = jnp.stack(
        [jnp.sum(result * result), jnp.sum(attn_out * attn_out), jnp.sum(ffn_out * ffn_out)]
    )
    packed = jnp.concatenate(
        [gain_one, gain_att, gain_two, bias_one, bias_att, bias_two,
         mid_gain_grad, mid_bias_grad, scale_grad, squares]
    )
    total = lax.psum(packed, ("ctx", "fsdp"))
    gain_grad = part_of(total[: 3 * width].reshape(3, width), 0, me, size, 1)
    bias_grad = part_of(total[3 * width : 6 * width].reshape(3, width), 0, me, size, 1)
    at = 6 * width
    mid_gain_sum = part_of(total[at : at + hidden_width], 0, me, size, 0)
    at = at + hidden_width
    mid_bias_sum = part_of(total[at : at + hidden_width], 0, me, size, 0)
    at = at + hidden_width
    scale_sum = part_of(total[at : at + HEADS], 0, me, size, 0)
    rms_values = jnp.sqrt(total[at + HEADS :] / (rows * groups * size * width))
    return (
        result.astype(low)[None],
        input_grad,
        qkv_sum.astype(f32),
        out_sum.astype(f32),
        fc1_sum.astype(f32),
        fc2_sum.astype(f32),
        gain_grad,
        bias_grad,
        mid_gain_sum,
        mid_bias_sum,
        scale_sum,
        rms_values,
    )


def solution(mesh):
    split = P("fsdp", "ctx", None)
    by_row = P("fsdp", None)
    by_col = P(None, "fsdp")
    one = P("fsdp")
    return jax.shard_map(
        local,
        mesh=mesh,
        in_specs=(split, split, by_row, by_row, by_row, by_row, by_row, by_col, by_col, one, one, one),
        out_specs=(split, split, by_row, by_row, by_row, by_row, by_col, by_col, one, one, one, P()),
        check_vma=False,
    )
```

```python
from functools import partial

import jax
import jax.numpy as jnp
from jax import lax
from jax.experimental import pallas as pl
from jax.experimental.pallas import tpu as pltpu
from jax.sharding import PartitionSpec as P

HEADS = 16
HEAD_DIM = 64
TILE = 256
EPS = 1e-05
MASKED = -1e30
SCALE = HEAD_DIM ** (-0.5)


def dot(a, b, ca=1, cb=0):
    return lax.dot_general(a, b, (((ca,), (cb,)), ((), ())), preferred_element_type=jnp.float32)


def normalize(values):
    centered = values - jnp.mean(values, axis=-1, keepdims=True)
    inverse = lax.rsqrt(jnp.mean(centered * centered, axis=-1, keepdims=True) + EPS)
    return (centered * inverse, inverse)


def norm_backward(grad_out, normed, inverse, gain_vec):
    grad_normed = grad_out * gain_vec
    grad_in = inverse * (
        grad_normed
        - jnp.mean(grad_normed, axis=-1, keepdims=True)
        - normed * jnp.mean(grad_normed * normed, axis=-1, keepdims=True)
    )
    return (grad_in, jnp.sum(grad_out * normed, axis=0), jnp.sum(grad_out, axis=0))


def sorted_sources(n_tiles):
    return [(t, 0) for t in range(n_tiles)] + [(t, 1) for t in range(n_tiles - 1, -1, -1)]


def pair_up(first, second):
    lane = lax.broadcasted_iota(jnp.int32, first[0].shape, 1)
    left = first[0] if first[1] == 0 else pltpu.roll(first[0], 64, 1)
    right = second[0] if second[1] == 1 else pltpu.roll(second[0], 64, 1)
    return jnp.where(lane < 64, left, right)


def sort_tiles(load, n_tiles, store):
    order = sorted_sources(n_tiles)
    for u in range(n_tiles):
        (ta, ha), (tb, hb) = order[2 * u], order[2 * u + 1]
        store(u, pair_up((load(ta), ha), (load(tb), hb)))


def unsort_tiles(load, n_tiles, store):
    for t in range(n_tiles):
        a, b = t, 2 * n_tiles - 1 - t
        store(t, pair_up((load(a // 2), a % 2), (load(b // 2), b % 2)))


def tile_spans(info_ref, qt, n_q_tiles, half_run, total_blocks):
    group = info_ref[0]
    per_run = n_q_tiles // 2
    low_first = group * half_run
    high_first = total_blocks * 64 - (group + 1) * half_run
    q_first = jnp.where(qt < per_run, low_first + qt * TILE, high_first + (qt - per_run) * TILE)
    start = jnp.int32(0)
    floor_first = jnp.int32(0)
    for d in range(8):
        floor_first = jnp.where(start <= q_first, start, floor_first)
        start = start + info_ref[1 + d]
    return q_first, floor_first // TILE


def query_rows(info_ref, q_first):
    q_pos = q_first + lax.broadcasted_iota(jnp.int32, (1, TILE), 1)
    start = jnp.int32(0)
    floor = jnp.zeros((1, TILE), jnp.int32)
    for d in range(8):
        floor = jnp.where(q_pos >= start, start, floor)
        start = start + info_ref[1 + d]
    return q_pos, floor


def usable_mask(q_pos, floor, kt):
    k_pos = kt * TILE + lax.broadcasted_iota(jnp.int32, (TILE, TILE), 0)
    return (k_pos <= q_pos) & (k_pos >= floor)


def attend_kernel(
    info_ref, hs_ref, q_ref, kv_ref, scaled_ref, att_ref, log_ref, qs_ref, ks_ref, vs_ref, kn_ref,
    *, n_q, n_k, k_at,
):
    per = TILE // 128
    f32 = jnp.float32

    def put(ref):
        def store(u, tile):
            ref[u // per, :, (u % per) * 128 : (u % per) * 128 + 128] = tile.astype(jnp.bfloat16)
        return store

    sort_tiles(lambda t: q_ref[t, 0].astype(f32), n_q, put(qs_ref))
    sort_tiles(lambda t: kv_ref[t, k_at].astype(f32), n_k, put(ks_ref))
    sort_tiles(lambda t: kv_ref[t, k_at + 1].astype(f32), n_k, put(vs_ref))
    for kt in range(n_k // per):
        kn_ref[kt] = ks_ref[kt].astype(f32).T.astype(jnp.bfloat16)

    def one_query_tile(qt, carry):
        q_first, k_low = tile_spans(info_ref, qt, n_q // per, n_q * 64, 2 * n_k)
        q_pos, floor = query_rows(info_ref, q_first)
        q_t = qs_ref[qt]

        def one_key_tile(kt, state):
            high, total, acc = state
            scores = dot(kn_ref[kt], q_t) * SCALE
            usable = usable_mask(q_pos, floor, kt)
            scores = jnp.where(usable, scores, MASKED)
            new_high = jnp.maximum(high, jnp.max(scores, axis=0, keepdims=True))
            probs = jnp.where(usable, jnp.exp(scores - new_high), 0.0)
            fix = jnp.exp(high - new_high)
            total = total * fix + jnp.sum(probs, axis=0, keepdims=True)
            acc = acc * fix + dot(vs_ref[kt], probs.astype(jnp.bfloat16))
            return new_high, total, acc

        high, total, acc = lax.fori_loop(
            k_low,
            q_first // TILE + 1,
            one_key_tile,
            (
                jnp.full((1, TILE), MASKED, f32),
                jnp.zeros((1, TILE), f32),
                jnp.zeros((HEAD_DIM, TILE), f32),
            ),
        )
        att_ref[qt] = acc / total
        log_ref[qt] = high + jnp.log(total)
        return carry

    lax.fori_loop(0, n_q // per, one_query_tile, 0)
    head_scale = hs_ref[0]

    def load(u):
        return att_ref[u // per, :, (u % per) * 128 : (u % per) * 128 + 128]

    def give(t, tile):
        scaled_ref[t] = (tile * head_scale).astype(jnp.bfloat16)

    unsort_tiles(load, n_q, give)


def attend_back_kernel(
    info_ref, qs_ref, ks_ref, vs_ref, att_ref, log_ref, go_ref, dq_ref, dk_ref, dv_ref, dsum_ref,
    go_s, kn_ref, vn_ref, dq_s, dk_s, dv_s,
    *, n_q, n_k,
):
    per = TILE // 128
    f32 = jnp.float32
    low = jnp.bfloat16

    def store(u, tile):
        go_s[u // per, :, (u % per) * 128 : (u % per) * 128 + 128] = tile.astype(low)

    sort_tiles(lambda t: go_ref[t].astype(f32), n_q, store)
    for kt in range(n_k // per):
        kn_ref[kt] = ks_ref[kt].astype(f32).T.astype(low)
        vn_ref[kt] = vs_ref[kt].astype(f32).T.astype(low)
        dk_s[kt] = jnp.zeros((TILE, HEAD_DIM), f32)
        dv_s[kt] = jnp.zeros((TILE, HEAD_DIM), f32)
    dsum_ref[...] = jnp.zeros((1, TILE), f32)

    def one_query_tile(qt, carry):
        q_first, k_low = tile_spans(info_ref, qt, n_q // per, n_q * 64, 2 * n_k)
        q_pos, floor = query_rows(info_ref, q_first)
        q_t = qs_ref[qt]
        g_t = go_s[qt]
        q_n = q_t.astype(f32).T.astype(low)
        g_n = g_t.astype(f32).T.astype(low)
        log_total = log_ref[qt]
        delta = jnp.sum(g_t.astype(f32) * att_ref[qt], axis=0, keepdims=True)
        dsum_ref[...] += delta

        def one_key_tile(kt, acc):
            scores = dot(kn_ref[kt], q_t) * SCALE
            usable = usable_mask(q_pos, floor, kt)
            probs = jnp.where(usable, jnp.exp(scores - log_total), 0.0)
            grad_probs = dot(vn_ref[kt], g_t)
            grad_scores = (probs * (grad_probs - delta)).astype(low)
            dv_s[kt] += dot(probs.astype(low), g_n)
            dk_s[kt] += dot(grad_scores, q_n)
            return acc + dot(ks_ref[kt], grad_scores)

        dq_s[qt] = lax.fori_loop(
            k_low, q_first // TILE + 1, one_key_tile, jnp.zeros((HEAD_DIM, TILE), f32)
        )
        return carry

    lax.fori_loop(0, n_q // per, one_query_tile, 0)

    def load_q(u):
        return dq_s[u // per, :, (u % per) * 128 : (u % per) * 128 + 128]

    def give_q(t, tile):
        dq_ref[t] = (tile * SCALE).astype(dq_ref.dtype)

    def load_k(u):
        return dk_s[u // per, (u % per) * 128 : (u % per) * 128 + 128, :].T

    def give_k(t, tile):
        dk_ref[t] = (tile * SCALE).astype(dk_ref.dtype)

    def load_v(u):
        return dv_s[u // per, (u % per) * 128 : (u % per) * 128 + 128, :].T

    def give_v(t, tile):
        dv_ref[t] = tile.astype(dv_ref.dtype)

    unsort_tiles(load_q, n_q, give_q)
    unsort_tiles(load_k, n_k, give_k)
    unsort_tiles(load_v, n_k, give_v)


def head_grad_kernel(x_ref, dq_ref, dk_ref, dv_ref, m_ref, c_ref, *, n_q):
    low, f32 = jnp.bfloat16, jnp.float32
    m_ref[...] = jnp.zeros(m_ref.shape, f32)
    c_ref[...] = jnp.zeros(c_ref.shape, f32)
    ones = jnp.ones((8, 256), low)

    def two_tiles(u, carry):
        x = jnp.concatenate([x_ref[2 * u], x_ref[2 * u + 1]], axis=0).astype(f32)
        normed = normalize(x)[0].astype(low)
        grads = jnp.concatenate(
            [
                jnp.concatenate([ref[2 * u], ref[2 * u + 1]], axis=1)
                for ref in (dq_ref, dk_ref, dv_ref)
            ],
            axis=0,
        )
        m_ref[...] += dot(grads, normed)
        c_ref[...] += dot(ones, grads, 1, 1)
        return carry

    lax.fori_loop(0, n_q // 2, two_tiles, 0)


def on_chip(n):
    return [pl.BlockSpec(memory_space=pltpu.VMEM)] * n


def in_scalars(n):
    return [pl.BlockSpec(memory_space=pltpu.SMEM)] * n


def attend(info, head_scale, q_tiles, kv_tiles, k_at):
    n_q, n_k = q_tiles.shape[0], kv_tiles.shape[0]
    nq, nk = n_q * 128 // TILE, n_k * 128 // TILE
    low, f32 = jnp.bfloat16, jnp.float32
    return pl.pallas_call(
        partial(attend_kernel, n_q=n_q, n_k=n_k, k_at=k_at),
        in_specs=in_scalars(2) + on_chip(2),
        out_specs=tuple(on_chip(6)),
        out_shape=(
            jax.ShapeDtypeStruct((n_q, HEAD_DIM, 128), low),
            jax.ShapeDtypeStruct((nq, HEAD_DIM, TILE), f32),
            jax.ShapeDtypeStruct((nq, 1, TILE), f32),
            jax.ShapeDtypeStruct((nq, HEAD_DIM, TILE), low),
            jax.ShapeDtypeStruct((nk, HEAD_DIM, TILE), low),
            jax.ShapeDtypeStruct((nk, HEAD_DIM, TILE), low),
        ),
        scratch_shapes=[pltpu.VMEM((nk, TILE, HEAD_DIM), low)],
        compiler_params=pltpu.CompilerParams(vmem_limit_bytes=48 << 20),
        name="attend",
    )(info, head_scale, q_tiles, kv_tiles)


def attend_back(info, qs, ks, vs, att, log_total, grad_tiles, kv_type):
    n_q = grad_tiles.shape[0]
    nq, nk = qs.shape[0], ks.shape[0]
    n_k = nk * TILE // 128
    low, f32 = jnp.bfloat16, jnp.float32
    return pl.pallas_call(
        partial(attend_back_kernel, n_q=n_q, n_k=n_k),
        in_specs=in_scalars(1) + on_chip(6),
        out_specs=tuple(on_chip(4)),
        out_shape=(
            jax.ShapeDtypeStruct((n_q, HEAD_DIM, 128), low),
            jax.ShapeDtypeStruct((n_k, HEAD_DIM, 128), kv_type),
            jax.ShapeDtypeStruct((n_k, HEAD_DIM, 128), kv_type),
            jax.ShapeDtypeStruct((1, TILE), f32),
        ),
        scratch_shapes=[
            pltpu.VMEM((nq, HEAD_DIM, TILE), low),
            pltpu.VMEM((nk, TILE, HEAD_DIM), low),
            pltpu.VMEM((nk, TILE, HEAD_DIM), low),
            pltpu.VMEM((nq, HEAD_DIM, TILE), f32),
            pltpu.VMEM((nk, TILE, HEAD_DIM), f32),
            pltpu.VMEM((nk, TILE, HEAD_DIM), f32),
        ],
        compiler_params=pltpu.CompilerParams(vmem_limit_bytes=48 << 20),
        name="attend_back",
    )(info, qs, ks, vs, att, log_total, grad_tiles)


def head_grad(x_tiles, dq, dk, dv):
    n_q, _, width = x_tiles.shape
    f32 = jnp.float32
    return pl.pallas_call(
        partial(head_grad_kernel, n_q=n_q),
        in_specs=on_chip(4),
        out_specs=tuple(on_chip(2)),
        out_shape=(
            jax.ShapeDtypeStruct((3 * HEAD_DIM, width), f32),
            jax.ShapeDtypeStruct((8, 3 * HEAD_DIM), f32),
        ),
        compiler_params=pltpu.CompilerParams(vmem_limit_bytes=48 << 20),
        name="head_grad",
    )(x_tiles, dq, dk, dv)


def place_sums_kernel(at_a_ref, at_b_ref, a_ref, b_ref, fc1_ref, out_ref, small_ref):
    f32 = jnp.float32
    cut_at = a_ref.shape[2]
    rest = fc1_ref.shape[2] - cut_at
    width = out_ref.shape[2]
    fc1_ref[0, :, :cut_at] = a_ref[0].astype(f32)
    fc1_ref[0, :, cut_at:] = b_ref[0, :, :rest].astype(f32)
    out_ref[0] = b_ref[0, :, rest : rest + width].astype(f32)
    small_ref[0] = b_ref[0, :, rest + width :].astype(f32)


def place_sums(at_a, at_b, sum_a, sum_b, hidden_width, width):
    blocks, n, wide_a = sum_a.shape
    wide_b = sum_b.shape[2]
    small = wide_a + wide_b - hidden_width - width
    f32 = jnp.float32

    def out_block(w):
        return pl.BlockSpec((1, n, w), lambda r, at_a_ref, at_b_ref: (r, 0, 0))

    return pl.pallas_call(
        place_sums_kernel,
        grid_spec=pltpu.PrefetchScalarGridSpec(
            num_scalar_prefetch=2,
            grid=(blocks,),
            in_specs=[
                pl.BlockSpec((1, n, wide_a), lambda r, at_a_ref, at_b_ref: (at_a_ref[r], 0, 0)),
                pl.BlockSpec((1, n, wide_b), lambda r, at_a_ref, at_b_ref: (at_b_ref[r], 0, 0)),
            ],
            out_specs=(out_block(hidden_width), out_block(width), out_block(small)),
        ),
        out_shape=(
            jax.ShapeDtypeStruct((blocks, n, hidden_width), f32),
            jax.ShapeDtypeStruct((blocks, n, width), f32),
            jax.ShapeDtypeStruct((blocks, n, small), f32),
        ),
        name="place_sums",
    )(at_a, at_b, sum_a, sum_b)


def place_qkv_kernel(
    at_l_ref, at_r_ref, left_ref, right_ref, weight_ref, gain_ref, bias_ref,
    grad_ref, gain_sum_ref, bias_sum_ref, scale_ref,
):
    f32 = jnp.float32
    block = pl.program_id(0)
    per = HEADS // 2
    which = block // per
    first = 2 * (block % per)
    n_rows = 3 * HEAD_DIM
    half = left_ref.shape[2]
    row = lax.broadcasted_iota(jnp.int32, (16, 128), 0)
    lane = lax.broadcasted_iota(jnp.int32, (1, 128), 1)

    def extra_row(head, i):
        rows = left_ref[at_l_ref[head], n_rows : n_rows + 16, :128].astype(f32)
        return jnp.sum(jnp.where((row == i) | (row == i + 4), rows, 0.0), axis=0, keepdims=True)

    @pl.when(block == 0)
    def _():
        gain_sum_ref[...] = jnp.zeros(gain_sum_ref.shape, f32)
        bias_sum_ref[...] = jnp.zeros(bias_sum_ref.shape, f32)
        for head in range(HEADS):
            scale_ref[head : head + 1, :] = extra_row(head, 3)

    columns = jnp.where(lane < HEAD_DIM, extra_row(first, which), extra_row(first + 1, which))
    rows = pl.ds(pl.multiple_of(which * HEAD_DIM, HEAD_DIM), HEAD_DIM)
    for side, (ref, at_ref) in enumerate(((left_ref, at_l_ref), (right_ref, at_r_ref))):
        sums = jnp.concatenate(
            [ref[at_ref[first], rows, :], ref[at_ref[first + 1], rows, :]], axis=0
        ).astype(f32).T
        d = slice(side * half, side * half + half)
        weight = weight_ref[d, :].astype(f32)
        grad_ref[d, :] = sums * gain_ref[d, :] + bias_ref[d, :] * columns
        gain_sum_ref[d, :] += weight * sums
        bias_sum_ref[d, :] += weight * columns


def place_qkv(at_l, at_r, left, right, weight, gain, bias):
    wide, n_columns = weight.shape
    f32 = jnp.float32

    def whole(shape):
        return pl.BlockSpec(shape, lambda i, at_l_ref, at_r_ref: (0,) * len(shape))

    column = pl.BlockSpec((wide, 128), lambda i, at_l_ref, at_r_ref: (0, i))
    return pl.pallas_call(
        place_qkv_kernel,
        grid_spec=pltpu.PrefetchScalarGridSpec(
            num_scalar_prefetch=2,
            grid=(n_columns // 128,),
            in_specs=[
                whole(left.shape), whole(right.shape), column, whole((wide, 1)), whole((wide, 1)),
            ],
            out_specs=(column, whole((wide, 128)), whole((wide, 128)), whole((HEADS, 128))),
        ),
        out_shape=(
            jax.ShapeDtypeStruct((wide, n_columns), f32),
            jax.ShapeDtypeStruct((wide, 128), f32),
            jax.ShapeDtypeStruct((wide, 128), f32),
            jax.ShapeDtypeStruct((HEADS, 128), f32),
        ),
        compiler_params=pltpu.CompilerParams(vmem_limit_bytes=48 << 20),
        name="place_qkv",
    )(at_l, at_r, left, right, weight, gain[:, None], bias[:, None])


def from_member(value, s, size):
    return lax.ppermute(value, "fsdp", [((i + s) % size, i) for i in range(size)])


def gather_parts(shard, size):
    return [shard] + [from_member(shard, s, size) for s in range(1, size)]


def part_of(value, s, me, size, axis):
    width = value.shape[axis] // size
    return lax.dynamic_slice_in_dim(value, ((me + s) % size) * width, width, axis)


def natural(parts, me, axis):
    size = len(parts)
    twice = jnp.concatenate(parts + parts, axis=axis)
    width = parts[0].shape[axis]
    return lax.dynamic_slice_in_dim(twice, ((size - me) % size) * width, size * width, axis)


def times_parts(value, parts, me):
    size = len(parts)
    total = dot(part_of(value, 0, me, size, 1), parts[0])
    for s in range(1, size):
        total = total + dot(part_of(value, s, me, size, 1), parts[s])
    return total


def all_tokens(value, size):
    return jnp.concatenate([value] + [from_member(value, s, size) for s in range(1, size)], axis=0)


def all_tokens_own(value, me, size):
    pieces = [part_of(value, 0, me, size, 1)]
    for s in range(1, size):
        pieces.append(from_member(part_of(value, size - s, me, size, 1), s, size))
    return jnp.concatenate(pieces, axis=0)


def swapped(value, stride, groups):
    return lax.ppermute(value, "ctx", [(i, i ^ stride) for i in range(groups)])


def half_of(value, which, axis=0):
    n = value.shape[axis] // 2
    return lax.dynamic_slice_in_dim(value, which * n, n, axis)


def bit_of(member, stride):
    return (member // stride) % 2


def plane_sum(product, sent, strides, member, groups):
    low, f32 = jnp.bfloat16, jnp.float32
    got = swapped(sent, strides[0], groups)
    total = (product(bit_of(member, strides[0])) + got.astype(f32)).astype(low)
    for stride in strides[1:]:
        bit = bit_of(member, stride)
        got = swapped(half_of(total, 1 - bit), stride, groups)
        total = (half_of(total, bit).astype(f32) + got.astype(f32)).astype(low)
    return total


def plane_join(value, strides, groups):
    for stride in strides:
        value = jnp.concatenate([value, swapped(value, stride, groups)], axis=0)
    return value


def from_line(value, k, plane, groups):
    return lax.ppermute(value, "ctx", [(i, (i + k * plane) % groups) for i in range(groups)])


def line_sum(value, line, plane, groups):
    lines = groups // plane
    n = value.shape[0] // lines
    total = lax.dynamic_slice_in_dim(value, line * n, n, 0).astype(jnp.float32)
    for k in range(1, lines):
        chunk = lax.dynamic_slice_in_dim(value, ((line + k) % lines) * n, n, 0)
        total = total + from_line(chunk, k, plane, groups).astype(jnp.float32)
    return total.astype(value.dtype)


def line_join(value, plane, groups):
    pieces = [value] + [from_line(value, k, plane, groups) for k in range(1, groups // plane)]
    return jnp.concatenate(pieces, axis=0)


def joined_places(lines_of, bits_of, order, member, line, lines, plane):
    place = (line - lines_of) % lines
    step = lines
    for i in order:
        place = place + (bits_of[i] ^ bit_of(member, 1 << i)) * step
        step = 2 * step
    return place.astype(jnp.int32)


def local(
    inputs, cotangent, doc_lengths, qkv_weight, out_weight, fc1_weight, fc2_weight,
    norm_gain, norm_bias, mid_gain, mid_bias, head_scale,
):
    low, f32 = jnp.bfloat16, jnp.float32
    groups = lax.axis_size("ctx")
    size = lax.axis_size("fsdp")
    member = lax.axis_index("ctx")
    me = lax.axis_index("fsdp")
    x_low = inputs[0]
    rows, width = x_low.shape
    hidden_width = fc1_weight.shape[1]
    copies = groups // HEADS
    head_groups = [[g * HEADS + i for i in range(HEADS)] for g in range(copies)]
    copy_groups = [[g * HEADS + i for g in range(copies)] for i in range(HEADS)]
    head = member % HEADS
    lines = 1
    while lines * lines < groups:
        lines = 2 * lines
    plane = groups // lines
    line = member // plane
    strides = [1 << i for i in range(plane.bit_length() - 1)]
    info = jnp.concatenate([(member // HEADS)[None].astype(jnp.int32), doc_lengths[0]])

    x_tiles = lax.all_gather(
        x_low, "ctx", axis=0, axis_index_groups=None if copies == 1 else head_groups
    )
    qkv_parts = gather_parts(qkv_weight, size)
    small = jnp.concatenate(
        [norm_gain.reshape(-1), norm_bias.reshape(-1), mid_gain, mid_bias, head_scale]
    )
    smalls = gather_parts(small, size)
    out_parts = gather_parts(out_weight, size)
    fc1_parts = gather_parts(fc1_weight, size)
    fc2_parts = gather_parts(fc2_weight, size)

    n_norm = norm_gain.size
    n_mid = mid_gain.size
    n_head = head_scale.size
    cut = [0, n_norm, 2 * n_norm, 2 * n_norm + n_mid, 2 * n_norm + 2 * n_mid, small.size]
    fields = [[s[cut[i] : cut[i + 1]] for s in smalls] for i in range(5)]
    gains = natural([f.reshape(3, -1) for f in fields[0]], me, 1).astype(f32)
    biases = natural([f.reshape(3, -1) for f in fields[1]], me, 1).astype(f32)
    mid_gains = natural(fields[2], me, 0).astype(f32)
    mid_biases = natural(fields[3], me, 0).astype(f32)
    head_scales = natural(fields[4], me, 0).astype(f32)
    my_scale = lax.dynamic_slice_in_dim(head_scales, head, 1, 0)

    x_local = x_low.astype(f32)
    norm_one, inv_one = normalize(x_local)
    normed_one = (norm_one * gains[0] + biases[0]).astype(low)
    project_t = sum(
        dot(qkv_parts[s], part_of(normed_one, s, me, size, 1), 0, 1) for s in range(size)
    ).astype(low)
    by_head = project_t.reshape(3, HEADS, HEAD_DIM, rows).transpose(1, 0, 2, 3)
    qkv_tiles = lax.all_to_all(by_head, "ctx", 0, 0, tiled=True, axis_index_groups=head_groups)
    if copies == 1:
        kv_tiles, k_at = qkv_tiles, 1
    else:
        kv_tiles, k_at = lax.all_gather(
            qkv_tiles[:, 1:], "ctx", axis=0, tiled=True, axis_index_groups=copy_groups
        ), 0
    scaled_tiles, att, log_total, qs, ks, vs = attend(info, my_scale, qkv_tiles, kv_tiles, k_at)
    scaled_t = lax.all_to_all(
        scaled_tiles, "ctx", 0, 0, tiled=True, axis_index_groups=head_groups
    ).reshape(width, rows)
    branch = sum(dot(part_of(scaled_t, s, me, size, 0), out_parts[s], 0, 0) for s in range(size))
    norm_att, inv_att = normalize(branch)
    attn_out = norm_att * gains[1] + biases[1]
    middle = x_local + attn_out
    norm_two, inv_two = normalize(middle)
    normed_two = (norm_two * gains[2] + biases[2]).astype(low)
    hidden = times_parts(normed_two, fc1_parts, me)
    active, gelu_back = jax.vjp(partial(jax.nn.gelu, approximate=True), hidden)
    norm_mid, inv_mid = normalize(active)
    mixed_in = (norm_mid * mid_gains + mid_biases).astype(low)
    ffn_out = times_parts(mixed_in, fc2_parts, me)
    result = middle + ffn_out

    grad_ffn = cotangent[0]
    grad_top = grad_ffn.astype(f32)
    fc2_grad = dot(all_tokens_own(mixed_in, me, size), all_tokens(grad_ffn, size), 0, 0).astype(low)
    grad_mixed = natural([dot(grad_ffn, part, 1, 1) for part in fc2_parts], me, 1)
    grad_active, mid_gain_grad, mid_bias_grad = norm_backward(
        grad_mixed, norm_mid, inv_mid, mid_gains
    )
    grad_hidden = gelu_back(grad_active)[0].astype(low)
    fc2_grad, grad_hidden = lax.optimization_barrier((fc2_grad, grad_hidden))
    fc2_sum = lax.psum(fc2_grad, "ctx")
    fc1_left = all_tokens_own(normed_two, me, size)
    fc1_right = all_tokens(grad_hidden, size)
    grad_two = natural([dot(grad_hidden, part, 1, 1) for part in fc1_parts], me, 1)
    grad_mid_in, gain_two, bias_two = norm_backward(grad_two, norm_two, inv_two, gains[2])
    grad_middle = grad_top + grad_mid_in
    grad_branch_f, gain_att, bias_att = norm_backward(grad_middle, norm_att, inv_att, gains[1])
    grad_branch = grad_branch_f.astype(low)
    out_left = all_tokens_own(scaled_t.T, me, size)
    out_right = all_tokens(grad_branch, size)

    squares = jnp.stack(
        [jnp.sum(result * result), jnp.sum(attn_out * attn_out), jnp.sum(ffn_out * ffn_out)]
    )
    norms = jnp.stack([gain_att, gain_two, bias_att, bias_two])
    mids = jnp.stack([mid_gain_grad, mid_bias_grad])

    def packed(s):
        return jnp.concatenate(
            [
                part_of(norms, s, me, size, 1).reshape(-1, 128),
                part_of(mids, s, me, size, 1).reshape(-1, 128),
                jnp.pad(squares[None], ((0, 7), (0, 125))),
            ],
            axis=0,
        )

    small_rows = packed(0)
    for s in range(1, size):
        small_rows = small_rows + from_member(packed(size - s), s, size)
    own_rows = fc1_weight.shape[0]
    n_small = small_rows.shape[0]
    small_block = jnp.concatenate([small_rows, jnp.zeros((own_rows - n_small, 128), f32)], axis=0)

    cut_at = 5 * hidden_width // 8

    def product_a(w):
        return dot(half_of(fc1_left, w, 1), fc1_right[:, :cut_at], 0, 0)

    def product_b(w):
        return jnp.concatenate(
            [
                dot(half_of(fc1_left, w, 1), fc1_right[:, cut_at:], 0, 0),
                dot(half_of(out_left, w, 1), out_right, 0, 0),
                half_of(small_block, w),
            ],
            axis=1,
        )

    sent_a = product_a(1 - bit_of(member, strides[0])).astype(low)
    sent_a, grad_branch = lax.optimization_barrier((sent_a, grad_branch))
    sent_b = product_b(1 - bit_of(member, strides[-1])).astype(low)

    grad_scaled_t = natural([dot(part, grad_branch, 1, 1) for part in out_parts], me, 0)
    grad_att = (
        grad_scaled_t.reshape(HEADS, HEAD_DIM, rows) * head_scales[:, None, None]
    ).astype(low)
    sent_b, grad_att = lax.optimization_barrier((sent_b, grad_att))
    sum_a = plane_sum(product_a, sent_a, strides, member, groups)
    sum_b = plane_sum(product_b, sent_b, strides[::-1], member, groups)
    both = line_sum(jnp.concatenate([sum_a, sum_b], axis=1), line, plane, groups)
    both = line_join(both, plane, groups)
    n_block = own_rows // groups
    bits = range(len(strides))
    block = jnp.arange(groups)
    block_bits = [block // lines // (1 << i) % 2 for i in bits]
    sum_a = plane_join(both[:, :cut_at], strides[::-1], groups).reshape(groups, n_block, -1)
    sum_b = plane_join(both[:, cut_at:], strides, groups).reshape(groups, n_block, -1)
    at_a = joined_places(
        block % lines, block_bits[::-1], bits[::-1], member, line, lines, plane
    )
    at_b = joined_places(block % lines, block_bits, bits, member, line, lines, plane)
    fc1_sum, out_sum, total = place_sums(at_a, at_b, sum_a, sum_b, hidden_width, width)
    fc1_sum = fc1_sum.reshape(own_rows, hidden_width)
    out_sum = out_sum.reshape(own_rows, width)
    total = total.reshape(own_rows, 128)[:n_small].reshape(-1)

    grad_tiles = lax.all_to_all(grad_att, "ctx", 0, 0, tiled=True, axis_index_groups=head_groups)
    dq, dk, dv, delta_sum = attend_back(
        info, qs, ks, vs, att, log_total, grad_tiles, low if copies == 1 else f32
    )
    if copies > 1:
        dk, dv = (
            lax.psum_scatter(
                d, "ctx", scatter_dimension=0, tiled=True, axis_index_groups=copy_groups
            ).astype(low)
            for d in (dk, dv)
        )

    head_sums, column_sums = head_grad(x_tiles, dq, dk, dv)
    my_scale_grad = jnp.sum(delta_sum) / my_scale[0]
    extra = jnp.concatenate(
        [column_sums[0].reshape(3, HEAD_DIM), jnp.full((1, HEAD_DIM), my_scale_grad)], axis=0
    )
    if copies > 1:
        head_sums, extra = (
            lax.psum(d, "ctx", axis_index_groups=copy_groups) for d in (head_sums, extra)
        )
    wide = norm_gain.shape[1]
    n_head_rows = head_sums.shape[0]
    extra = jnp.pad(jnp.concatenate([extra, extra], axis=1), ((0, 12), (0, wide - 2 * HEAD_DIM)))

    def with_extra(sums, more):
        high = more.astype(low)
        rest_of = (more - high.astype(f32)).astype(low)
        both_parts = high + jnp.roll(rest_of, 4, axis=0)
        return jnp.concatenate([sums.astype(low), both_parts], axis=0)

    own_sums = part_of(head_sums, 0, me, size, 1)
    own_extra = extra
    for s in range(1, size):
        got = from_member(
            with_extra(part_of(head_sums, size - s, me, size, 1), extra), s, size
        ).astype(f32)
        own_sums = own_sums + got[:n_head_rows]
        got = got[n_head_rows:]
        own_extra = own_extra + jnp.pad(got[:4] + got[4:8], ((0, 12), (0, 0)))
    payload = lax.optimization_barrier(with_extra(own_sums, own_extra))
    heads = jnp.arange(HEADS)
    if copies > 1:
        every = lax.all_gather(payload, "ctx", axis=0, axis_index_groups=head_groups)
        left, right = every[:, :, : wide // 2], every[:, :, wide // 2 :]
        at_l = at_r = heads.astype(jnp.int32)
    else:
        on_line = line_join(payload, plane, groups)
        left = plane_join(on_line[:, : wide // 2], strides, groups)
        right = plane_join(on_line[:, wide // 2 :], strides[::-1], groups)
        left, right = (d.reshape(HEADS, n_head_rows + 16, wide // 2) for d in (left, right))
        head_bits = [bit_of(heads, stride) for stride in strides]
        at_l = joined_places(heads // plane, head_bits, bits, member, line, lines, plane)
        at_r = joined_places(heads // plane, head_bits, bits[::-1], member, line, lines, plane)
    qkv_sum, gain_parts, bias_parts, scales = place_qkv(
        at_l, at_r, left, right, qkv_weight, norm_gain[0].astype(f32), norm_bias[0].astype(f32)
    )
    gain_one, bias_one = jnp.sum(gain_parts, axis=1), jnp.sum(bias_parts, axis=1)
    scale_sum = part_of(scales[:, 0], 0, me, size, 0)

    grads_out = jnp.stack([dq, dk, dv], axis=1)
    grad_proj_t = lax.all_to_all(
        grads_out, "ctx", 0, 0, tiled=True, axis_index_groups=head_groups
    ).transpose(1, 0, 2, 3).reshape(3 * width, rows)
    grad_one = natural([dot(grad_proj_t, part, 0, 1) for part in qkv_parts], me, 1)
    grad_first = norm_backward(grad_one, norm_one, inv_one, gains[0])[0]
    input_grad = (grad_middle + grad_first).astype(low)[None]

    own_norms = total[: 4 * wide].reshape(4, wide)
    gain_grad = jnp.stack([gain_one, own_norms[0], own_norms[1]])
    bias_grad = jnp.stack([bias_one, own_norms[2], own_norms[3]])
    at = 4 * wide
    n_own = mid_gain.shape[0]
    mid_gain_sum = total[at : at + n_own]
    mid_bias_sum = total[at + n_own : at + 2 * n_own]
    at = at + 2 * n_own
    rms_values = jnp.sqrt(total[at : at + 3] / (rows * groups * size * width))
    return (
        result.astype(low)[None],
        input_grad,
        qkv_sum,
        out_sum,
        fc1_sum,
        fc2_sum.astype(f32),
        gain_grad,
        bias_grad,
        mid_gain_sum,
        mid_bias_sum,
        scale_sum,
        rms_values,
    )


def solution(mesh):
    split = P("fsdp", "ctx", None)
    by_row = P("fsdp", None)
    by_col = P(None, "fsdp")
    one = P("fsdp")
    return jax.shard_map(
        local,
        mesh=mesh,
        in_specs=(split, split, by_row, by_row, by_row, by_row, by_row, by_col, by_col, one, one, one),
        out_specs=(split, split, by_row, by_row, by_row, by_row, by_col, by_col, one, one, one, P()),
        check_vma=False,
    )
```

```python
from functools import partial

import jax
import jax.numpy as jnp
from jax import lax
from jax.experimental import pallas as pl
from jax.experimental.pallas import tpu as pltpu
from jax.sharding import PartitionSpec as P

HEADS = 16
HEAD_DIM = 64
TILE = 256
EPS = 1e-05
MASKED = -1e30
SCALE = HEAD_DIM ** (-0.5)


def dot(a, b, ca=1, cb=0):
    return lax.dot_general(a, b, (((ca,), (cb,)), ((), ())), preferred_element_type=jnp.float32)


def normalize(values):
    centered = values - jnp.mean(values, axis=-1, keepdims=True)
    inverse = lax.rsqrt(jnp.mean(centered * centered, axis=-1, keepdims=True) + EPS)
    return (centered * inverse, inverse)


def norm_backward(grad_out, normed, inverse, gain_vec):
    grad_normed = grad_out * gain_vec
    grad_in = inverse * (
        grad_normed
        - jnp.mean(grad_normed, axis=-1, keepdims=True)
        - normed * jnp.mean(grad_normed * normed, axis=-1, keepdims=True)
    )
    return (grad_in, jnp.sum(grad_out * normed, axis=0), jnp.sum(grad_out, axis=0))


def sorted_sources(n_tiles):
    return [(t, 0) for t in range(n_tiles)] + [(t, 1) for t in range(n_tiles - 1, -1, -1)]


def pair_up(first, second):
    lane = lax.broadcasted_iota(jnp.int32, first[0].shape, 1)
    left = first[0] if first[1] == 0 else pltpu.roll(first[0], 64, 1)
    right = second[0] if second[1] == 1 else pltpu.roll(second[0], 64, 1)
    return jnp.where(lane < 64, left, right)


def sort_tiles(load, n_tiles, store):
    order = sorted_sources(n_tiles)
    for u in range(n_tiles):
        (ta, ha), (tb, hb) = order[2 * u], order[2 * u + 1]
        store(u, pair_up((load(ta), ha), (load(tb), hb)))


def unsort_tiles(load, n_tiles, store):
    for t in range(n_tiles):
        a, b = t, 2 * n_tiles - 1 - t
        store(t, pair_up((load(a // 2), a % 2), (load(b // 2), b % 2)))


def tile_spans(info_ref, qt, n_q_tiles, half_run, total_blocks):
    group = info_ref[0]
    per_run = n_q_tiles // 2
    low_first = group * half_run
    high_first = total_blocks * 64 - (group + 1) * half_run
    q_first = jnp.where(qt < per_run, low_first + qt * TILE, high_first + (qt - per_run) * TILE)
    start = jnp.int32(0)
    floor_first = jnp.int32(0)
    for d in range(8):
        floor_first = jnp.where(start <= q_first, start, floor_first)
        start = start + info_ref[1 + d]
    return q_first, floor_first // TILE


def query_rows(info_ref, q_first):
    q_pos = q_first + lax.broadcasted_iota(jnp.int32, (1, TILE), 1)
    start = jnp.int32(0)
    floor = jnp.zeros((1, TILE), jnp.int32)
    for d in range(8):
        floor = jnp.where(q_pos >= start, start, floor)
        start = start + info_ref[1 + d]
    return q_pos, floor


def usable_mask(q_pos, floor, kt):
    k_pos = kt * TILE + lax.broadcasted_iota(jnp.int32, (TILE, TILE), 0)
    return (k_pos <= q_pos) & (k_pos >= floor)


def attend_kernel(
    info_ref, hs_ref, q_ref, kv_ref, scaled_ref, att_ref, log_ref, qs_ref, ks_ref, vs_ref, kn_ref,
    *, n_q, n_k, k_at,
):
    per = TILE // 128
    f32 = jnp.float32

    def put(ref):
        def store(u, tile):
            ref[u // per, :, (u % per) * 128 : (u % per) * 128 + 128] = tile.astype(jnp.bfloat16)
        return store

    sort_tiles(lambda t: q_ref[t, 0].astype(f32), n_q, put(qs_ref))
    sort_tiles(lambda t: kv_ref[t, k_at].astype(f32), n_k, put(ks_ref))
    sort_tiles(lambda t: kv_ref[t, k_at + 1].astype(f32), n_k, put(vs_ref))
    for kt in range(n_k // per):
        kn_ref[kt] = ks_ref[kt].astype(f32).T.astype(jnp.bfloat16)

    def one_query_tile(qt, carry):
        q_first, k_low = tile_spans(info_ref, qt, n_q // per, n_q * 64, 2 * n_k)
        q_pos, floor = query_rows(info_ref, q_first)
        q_t = qs_ref[qt]

        def one_key_tile(kt, state):
            high, total, acc = state
            scores = dot(kn_ref[kt], q_t) * SCALE
            usable = usable_mask(q_pos, floor, kt)
            scores = jnp.where(usable, scores, MASKED)
            new_high = jnp.maximum(high, jnp.max(scores, axis=0, keepdims=True))
            probs = jnp.where(usable, jnp.exp(scores - new_high), 0.0)
            fix = jnp.exp(high - new_high)
            total = total * fix + jnp.sum(probs, axis=0, keepdims=True)
            acc = acc * fix + dot(vs_ref[kt], probs.astype(jnp.bfloat16))
            return new_high, total, acc

        high, total, acc = lax.fori_loop(
            k_low,
            q_first // TILE + 1,
            one_key_tile,
            (
                jnp.full((1, TILE), MASKED, f32),
                jnp.zeros((1, TILE), f32),
                jnp.zeros((HEAD_DIM, TILE), f32),
            ),
        )
        att_ref[qt] = acc / total
        log_ref[qt] = high + jnp.log(total)
        return carry

    lax.fori_loop(0, n_q // per, one_query_tile, 0)
    head_scale = hs_ref[0]

    def load(u):
        return att_ref[u // per, :, (u % per) * 128 : (u % per) * 128 + 128]

    def give(t, tile):
        scaled_ref[t] = (tile * head_scale).astype(jnp.bfloat16)

    unsort_tiles(load, n_q, give)


def attend_back_kernel(
    info_ref, qs_ref, ks_ref, vs_ref, att_ref, log_ref, go_ref, dq_ref, dk_ref, dv_ref, dsum_ref,
    go_s, kn_ref, vn_ref, dq_s, dk_s, dv_s,
    *, n_q, n_k,
):
    per = TILE // 128
    f32 = jnp.float32
    low = jnp.bfloat16

    def store(u, tile):
        go_s[u // per, :, (u % per) * 128 : (u % per) * 128 + 128] = tile.astype(low)

    sort_tiles(lambda t: go_ref[t].astype(f32), n_q, store)
    for kt in range(n_k // per):
        kn_ref[kt] = ks_ref[kt].astype(f32).T.astype(low)
        vn_ref[kt] = vs_ref[kt].astype(f32).T.astype(low)
        dk_s[kt] = jnp.zeros((TILE, HEAD_DIM), f32)
        dv_s[kt] = jnp.zeros((TILE, HEAD_DIM), f32)
    dsum_ref[...] = jnp.zeros((1, TILE), f32)

    def one_query_tile(qt, carry):
        q_first, k_low = tile_spans(info_ref, qt, n_q // per, n_q * 64, 2 * n_k)
        q_pos, floor = query_rows(info_ref, q_first)
        q_t = qs_ref[qt]
        g_t = go_s[qt]
        q_n = q_t.astype(f32).T.astype(low)
        g_n = g_t.astype(f32).T.astype(low)
        log_total = log_ref[qt]
        delta = jnp.sum(g_t.astype(f32) * att_ref[qt], axis=0, keepdims=True)
        dsum_ref[...] += delta

        def one_key_tile(kt, acc):
            scores = dot(kn_ref[kt], q_t) * SCALE
            usable = usable_mask(q_pos, floor, kt)
            probs = jnp.where(usable, jnp.exp(scores - log_total), 0.0)
            grad_probs = dot(vn_ref[kt], g_t)
            grad_scores = (probs * (grad_probs - delta)).astype(low)
            dv_s[kt] += dot(probs.astype(low), g_n)
            dk_s[kt] += dot(grad_scores, q_n)
            return acc + dot(ks_ref[kt], grad_scores)

        dq_s[qt] = lax.fori_loop(
            k_low, q_first // TILE + 1, one_key_tile, jnp.zeros((HEAD_DIM, TILE), f32)
        )
        return carry

    lax.fori_loop(0, n_q // per, one_query_tile, 0)

    def load_q(u):
        return dq_s[u // per, :, (u % per) * 128 : (u % per) * 128 + 128]

    def give_q(t, tile):
        dq_ref[t] = (tile * SCALE).astype(dq_ref.dtype)

    def load_k(u):
        return dk_s[u // per, (u % per) * 128 : (u % per) * 128 + 128, :].T

    def give_k(t, tile):
        dk_ref[t] = (tile * SCALE).astype(dk_ref.dtype)

    def load_v(u):
        return dv_s[u // per, (u % per) * 128 : (u % per) * 128 + 128, :].T

    def give_v(t, tile):
        dv_ref[t] = tile.astype(dv_ref.dtype)

    unsort_tiles(load_q, n_q, give_q)
    unsort_tiles(load_k, n_k, give_k)
    unsort_tiles(load_v, n_k, give_v)


def head_grad_kernel(x_ref, dq_ref, dk_ref, dv_ref, m_ref, c_ref):
    low, f32 = jnp.bfloat16, jnp.float32

    @pl.when(pl.program_id(0) == 0)
    def _():
        m_ref[...] = jnp.zeros(m_ref.shape, f32)
        c_ref[...] = jnp.zeros(c_ref.shape, f32)

    x = jnp.concatenate([x_ref[0], x_ref[1]], axis=0).astype(f32)
    normed = normalize(x)[0].astype(low)
    grads = jnp.concatenate(
        [jnp.concatenate([ref[0], ref[1]], axis=1) for ref in (dq_ref, dk_ref, dv_ref)], axis=0
    )
    m_ref[...] += dot(grads, normed)
    c_ref[...] += dot(jnp.ones((8, grads.shape[1]), low), grads, 1, 1)


def takes(microseconds):
    return pl.CostEstimate(
        flops=0, transcendentals=0, bytes_accessed=int(microseconds * 3.2e6)
    )


def on_chip(n):
    return [pl.BlockSpec(memory_space=pltpu.VMEM)] * n


def in_scalars(n):
    return [pl.BlockSpec(memory_space=pltpu.SMEM)] * n


def attend(info, head_scale, q_tiles, kv_tiles, k_at):
    n_q, n_k = q_tiles.shape[0], kv_tiles.shape[0]
    nq, nk = n_q * 128 // TILE, n_k * 128 // TILE
    low, f32 = jnp.bfloat16, jnp.float32
    return pl.pallas_call(
        partial(attend_kernel, n_q=n_q, n_k=n_k, k_at=k_at),
        in_specs=in_scalars(2) + on_chip(2),
        out_specs=tuple(on_chip(6)),
        out_shape=(
            jax.ShapeDtypeStruct((n_q, HEAD_DIM, 128), low),
            jax.ShapeDtypeStruct((nq, HEAD_DIM, TILE), f32),
            jax.ShapeDtypeStruct((nq, 1, TILE), f32),
            jax.ShapeDtypeStruct((nq, HEAD_DIM, TILE), low),
            jax.ShapeDtypeStruct((nk, HEAD_DIM, TILE), low),
            jax.ShapeDtypeStruct((nk, HEAD_DIM, TILE), low),
        ),
        scratch_shapes=[pltpu.VMEM((nk, TILE, HEAD_DIM), low)],
        compiler_params=pltpu.CompilerParams(vmem_limit_bytes=48 << 20),
        cost_estimate=takes(10),
        name="attend",
    )(info, head_scale, q_tiles, kv_tiles)


def attend_back(info, qs, ks, vs, att, log_total, grad_tiles, kv_type):
    n_q = grad_tiles.shape[0]
    nq, nk = qs.shape[0], ks.shape[0]
    n_k = nk * TILE // 128
    low, f32 = jnp.bfloat16, jnp.float32
    return pl.pallas_call(
        partial(attend_back_kernel, n_q=n_q, n_k=n_k),
        in_specs=in_scalars(1) + on_chip(6),
        out_specs=tuple(on_chip(4)),
        out_shape=(
            jax.ShapeDtypeStruct((n_q, HEAD_DIM, 128), low),
            jax.ShapeDtypeStruct((n_k, HEAD_DIM, 128), kv_type),
            jax.ShapeDtypeStruct((n_k, HEAD_DIM, 128), kv_type),
            jax.ShapeDtypeStruct((1, TILE), f32),
        ),
        scratch_shapes=[
            pltpu.VMEM((nq, HEAD_DIM, TILE), low),
            pltpu.VMEM((nk, TILE, HEAD_DIM), low),
            pltpu.VMEM((nk, TILE, HEAD_DIM), low),
            pltpu.VMEM((nq, HEAD_DIM, TILE), f32),
            pltpu.VMEM((nk, TILE, HEAD_DIM), f32),
            pltpu.VMEM((nk, TILE, HEAD_DIM), f32),
        ],
        compiler_params=pltpu.CompilerParams(vmem_limit_bytes=48 << 20),
        cost_estimate=takes(10),
        name="attend_back",
    )(info, qs, ks, vs, att, log_total, grad_tiles)


def stream_tiles(gathered, which):
    _, _, rows, width = gathered.shape
    return pl.BlockSpec((2, pl.Squeezed(), rows, width), lambda i: (i, which, 0, 0))


def head_grad(gathered, dq, dk, dv):
    width = gathered.shape[3]
    f32 = jnp.float32
    tiles = pl.BlockSpec((2, HEAD_DIM, 128), lambda i: (i, 0, 0))
    return pl.pallas_call(
        head_grad_kernel,
        grid=(gathered.shape[0] // 2,),
        in_specs=[stream_tiles(gathered, 0)] + [tiles] * 3,
        out_specs=(
            pl.BlockSpec((3 * HEAD_DIM, width), lambda i: (0, 0)),
            pl.BlockSpec((8, 3 * HEAD_DIM), lambda i: (0, 0)),
        ),
        out_shape=(
            jax.ShapeDtypeStruct((3 * HEAD_DIM, width), f32),
            jax.ShapeDtypeStruct((8, 3 * HEAD_DIM), f32),
        ),
        cost_estimate=takes(8),
        name="head_grad",
    )(gathered, dq, dk, dv)


def place_sums_kernel(
    at_a_ref, at_b_ref, a_near_ref, a_far_ref, b_near_ref, b_far_ref, fc1_ref, out_ref
):
    f32 = jnp.float32
    per, n, hidden_width = fc1_ref.shape
    half = a_near_ref.shape[0]
    cut_at = a_near_ref.shape[2]
    rest = hidden_width - cut_at

    def put_a(i, ref, at):
        fc1_ref[i, :, :cut_at] = ref[at].astype(f32)

    def put_b(i, ref, at):
        fc1_ref[i, :, cut_at:] = ref[at, :, :rest].astype(f32)
        out_ref[i] = ref[at, :, rest:].astype(f32)

    for i in range(per):
        r = pl.program_id(0) * per + i
        for put, at, near, far in (
            (put_a, at_a_ref[r], a_near_ref, a_far_ref),
            (put_b, at_b_ref[r], b_near_ref, b_far_ref),
        ):
            pl.when(at < half)(partial(put, i, near, at))
            pl.when(at >= half)(partial(put, i, far, at - half))


def place_sums(at_a, at_b, sums_a, sums_b, hidden_width):
    half, n, wide_a = sums_a[0].shape
    wide_b = sums_b[0].shape[2]
    blocks = 2 * half
    per = 2
    width = wide_a + wide_b - hidden_width
    f32 = jnp.float32

    def out_block(w):
        return pl.BlockSpec((per, n, w), lambda r, at_a_ref, at_b_ref: (r, 0, 0))

    return pl.pallas_call(
        place_sums_kernel,
        grid_spec=pltpu.PrefetchScalarGridSpec(
            num_scalar_prefetch=2,
            grid=(blocks // per,),
            in_specs=on_chip(4),
            out_specs=(out_block(hidden_width), out_block(width)),
        ),
        out_shape=(
            jax.ShapeDtypeStruct((blocks, n, hidden_width), f32),
            jax.ShapeDtypeStruct((blocks, n, width), f32),
        ),
        compiler_params=pltpu.CompilerParams(vmem_limit_bytes=48 << 20),
        cost_estimate=takes(7),
        name="place_sums",
    )(at_a, at_b, *sums_a, *sums_b)


def place_qkv_kernel(
    at_l_ref, at_r_ref, left_ref, right_ref, weight_ref, gain_ref, bias_ref,
    grad_ref, gain_sum_ref, bias_sum_ref, scale_ref, small_ref,
):
    f32 = jnp.float32
    step = pl.program_id(0)
    n_rows = 3 * HEAD_DIM
    half = left_ref.shape[2]
    pairs = grad_ref.shape[1] // 128
    per = HEADS // 2 // pairs
    which = step // per
    row = lax.broadcasted_iota(jnp.int32, (16, 128), 0)
    lane = lax.broadcasted_iota(jnp.int32, (1, 128), 1)

    def extra_row(head, i):
        rows = left_ref[at_l_ref[head], n_rows : n_rows + 16, :128].astype(f32)
        return jnp.sum(jnp.where((row == i) | (row == i + 4), rows, 0.0), axis=0, keepdims=True)

    @pl.when(step == 0)
    def _():
        gain_sum_ref[...] = jnp.zeros(gain_sum_ref.shape, f32)
        bias_sum_ref[...] = jnp.zeros(bias_sum_ref.shape, f32)
        for side, ref in enumerate((left_ref, right_ref)):
            small_ref[:, side * half : side * half + half] = sum(
                ref[head, n_rows + 16 :, :].astype(f32) for head in range(HEADS)
            )
        for head in range(HEADS):
            scale_ref[head : head + 1, :] = extra_row(head, 3)

    rows = pl.ds(pl.multiple_of(which * HEAD_DIM, HEAD_DIM), HEAD_DIM)
    for pair in range(pairs):
        first = 2 * (step % per * pairs + pair)
        j = slice(pair * 128, pair * 128 + 128)
        columns = jnp.where(lane < HEAD_DIM, extra_row(first, which), extra_row(first + 1, which))
        for side, (ref, at_ref) in enumerate(((left_ref, at_l_ref), (right_ref, at_r_ref))):
            sums = jnp.concatenate(
                [ref[at_ref[first], rows, :], ref[at_ref[first + 1], rows, :]], axis=0
            ).astype(f32).T
            d = slice(side * half, side * half + half)
            weight = weight_ref[d, j].astype(f32)
            grad_ref[d, j] = sums * gain_ref[d, :] + bias_ref[d, :] * columns
            gain_sum_ref[d, :] += weight * sums
            bias_sum_ref[d, :] += weight * columns


def place_qkv(at_l, at_r, left, right, weight, gain, bias):
    wide, n_columns = weight.shape
    f32 = jnp.float32
    step = 512

    def whole(shape):
        return pl.BlockSpec(shape, lambda i, at_l_ref, at_r_ref: (0,) * len(shape))

    column = pl.BlockSpec((wide, step), lambda i, at_l_ref, at_r_ref: (0, i))
    outs = ((wide, 128), (wide, 128), (HEADS, 128), (16, wide))
    return pl.pallas_call(
        place_qkv_kernel,
        grid_spec=pltpu.PrefetchScalarGridSpec(
            num_scalar_prefetch=2,
            grid=(n_columns // step,),
            in_specs=[
                whole(left.shape), whole(right.shape), column, whole((wide, 1)), whole((wide, 1)),
            ],
            out_specs=(column,) + tuple(whole(shape) for shape in outs),
        ),
        out_shape=(jax.ShapeDtypeStruct((wide, n_columns), f32),)
        + tuple(jax.ShapeDtypeStruct(shape, f32) for shape in outs),
        compiler_params=pltpu.CompilerParams(vmem_limit_bytes=48 << 20),
        cost_estimate=takes(9),
        name="place_qkv",
    )(at_l, at_r, left, right, weight, gain[:, None], bias[:, None])


def from_member(value, s, size):
    return lax.ppermute(value, "fsdp", [((i + s) % size, i) for i in range(size)])


def gather_parts(shard, size):
    return [shard] + [from_member(shard, s, size) for s in range(1, size)]


def part_of(value, s, me, size, axis):
    width = value.shape[axis] // size
    return lax.dynamic_slice_in_dim(value, ((me + s) % size) * width, width, axis)


def natural(parts, me, axis):
    size = len(parts)
    twice = jnp.concatenate(parts + parts, axis=axis)
    width = parts[0].shape[axis]
    return lax.dynamic_slice_in_dim(twice, ((size - me) % size) * width, size * width, axis)


def times_parts(value, parts, me):
    size = len(parts)
    total = dot(part_of(value, 0, me, size, 1), parts[0])
    for s in range(1, size):
        total = total + dot(part_of(value, s, me, size, 1), parts[s])
    return total


def all_tokens(value, size):
    return jnp.concatenate([value] + [from_member(value, s, size) for s in range(1, size)], axis=0)


def all_tokens_own(value, me, size):
    pieces = [part_of(value, 0, me, size, 1)]
    for s in range(1, size):
        pieces.append(from_member(part_of(value, size - s, me, size, 1), s, size))
    return jnp.concatenate(pieces, axis=0)


def swapped(value, stride, groups):
    return lax.ppermute(value, "ctx", [(i, i ^ stride) for i in range(groups)])


def half_of(value, which, axis=0):
    n = value.shape[axis] // 2
    return lax.dynamic_slice_in_dim(value, which * n, n, axis)


def bit_of(member, stride):
    return (member // stride) % 2


def from_line(value, k, plane, groups):
    return lax.ppermute(value, "ctx", [(i, (i + k * plane) % groups) for i in range(groups)])


def joined_places(lines_of, bits_of, order, member, line, lines, plane):
    place = (line - lines_of) % lines
    step = lines
    for i in order:
        place = place + (bits_of[i] ^ bit_of(member, 1 << i)) * step
        step = 2 * step
    return place.astype(jnp.int32)


def local(
    inputs, cotangent, doc_lengths, qkv_weight, out_weight, fc1_weight, fc2_weight,
    norm_gain, norm_bias, mid_gain, mid_bias, head_scale,
):
    low, f32 = jnp.bfloat16, jnp.float32
    groups = lax.axis_size("ctx")
    size = lax.axis_size("fsdp")
    member = lax.axis_index("ctx")
    me = lax.axis_index("fsdp")
    x_low = inputs[0]
    rows, width = x_low.shape
    hidden_width = fc1_weight.shape[1]
    copies = groups // HEADS
    head_groups = [[g * HEADS + i for i in range(HEADS)] for g in range(copies)]
    copy_groups = [[g * HEADS + i for g in range(copies)] for i in range(HEADS)]
    head = member % HEADS
    lines = 1
    while lines * lines < groups:
        lines = 2 * lines
    plane = groups // lines
    line = member // plane
    strides = [1 << i for i in range(plane.bit_length() - 1)]
    info = jnp.concatenate([(member // HEADS)[None].astype(jnp.int32), doc_lengths[0]])

    gathered = lax.all_gather(
        x_low[None],
        "ctx", axis=0, axis_index_groups=None if copies == 1 else head_groups,
    )
    norm_vecs = jnp.concatenate([norm_gain, norm_bias], axis=0)
    norm_vecs = natural(gather_parts(norm_vecs, size), me, 1).astype(f32)
    norm_vecs, qkv_shard = lax.optimization_barrier((norm_vecs, qkv_weight))
    gains, biases = norm_vecs[:3], norm_vecs[3:]
    qkv_parts = gather_parts(qkv_shard, size)

    x_local = x_low.astype(f32)
    norm_one, inv_one = normalize(x_local)
    normed_one = (norm_one * gains[0] + biases[0]).astype(low)
    normed_one, small, out_shard, fc1_shard, fc2_shard = lax.optimization_barrier(
        (
            normed_one, jnp.concatenate([mid_gain, mid_bias, head_scale]),
            out_weight, fc1_weight, fc2_weight,
        )
    )
    smalls = gather_parts(small, size)
    out_parts = gather_parts(out_shard, size)
    fc1_parts = gather_parts(fc1_shard, size)
    fc2_parts = gather_parts(fc2_shard, size)
    n_mid = mid_gain.size
    cut = [0, n_mid, 2 * n_mid, small.size]
    mid_gains, mid_biases, head_scales = (
        natural([v[cut[i] : cut[i + 1]] for v in smalls], me, 0).astype(f32) for i in range(3)
    )
    my_scale = lax.dynamic_slice_in_dim(head_scales, head, 1, 0)
    project_t = sum(
        dot(qkv_parts[s], part_of(normed_one, s, me, size, 1), 0, 1) for s in range(size)
    ).astype(low)
    by_head = project_t.reshape(3, HEADS, HEAD_DIM, rows).transpose(1, 0, 2, 3)
    qkv_tiles = lax.all_to_all(by_head, "ctx", 0, 0, tiled=True, axis_index_groups=head_groups)
    if copies == 1:
        kv_tiles, k_at = qkv_tiles, 1
    else:
        kv_tiles, k_at = lax.all_gather(
            qkv_tiles[:, 1:], "ctx", axis=0, tiled=True, axis_index_groups=copy_groups
        ), 0
    scaled_tiles, att, log_total, qs, ks, vs = attend(info, my_scale, qkv_tiles, kv_tiles, k_at)
    scaled_t = lax.all_to_all(
        scaled_tiles, "ctx", 0, 0, tiled=True, axis_index_groups=head_groups
    ).reshape(width, rows)
    branch = sum(dot(part_of(scaled_t, s, me, size, 0), out_parts[s], 0, 0) for s in range(size))
    norm_att, inv_att = normalize(branch)
    attn_out = norm_att * gains[1] + biases[1]
    middle = x_local + attn_out
    norm_two, inv_two = normalize(middle)
    normed_two = (norm_two * gains[2] + biases[2]).astype(low)
    hidden = times_parts(normed_two, fc1_parts, me)
    active, gelu_back = jax.vjp(partial(jax.nn.gelu, approximate=True), hidden)
    norm_mid, inv_mid = normalize(active)
    mixed_in = (norm_mid * mid_gains + mid_biases).astype(low)
    ffn_out = times_parts(mixed_in, fc2_parts, me)
    result = middle + ffn_out

    grad_ffn = cotangent[0]
    grad_top = grad_ffn.astype(f32)
    fc2_grad = dot(
        all_tokens_own(mixed_in, me, size), all_tokens(grad_ffn, size), 0, 0
    ).astype(low)
    fc2_grad, norm_mid = lax.optimization_barrier((fc2_grad, norm_mid))
    fc2_sum = lax.psum(fc2_grad, "ctx")
    grad_mixed = natural([dot(grad_ffn, part, 1, 1) for part in fc2_parts], me, 1)
    grad_active, mid_gain_grad, mid_bias_grad = norm_backward(
        grad_mixed, norm_mid, inv_mid, mid_gains
    )
    grad_hidden = gelu_back(grad_active)[0].astype(low)
    fc1_left = all_tokens_own(normed_two, me, size)
    fc1_right = all_tokens(grad_hidden, size)
    grad_two = natural([dot(grad_hidden, part, 1, 1) for part in fc1_parts], me, 1)
    grad_mid_in, gain_two, bias_two = norm_backward(grad_two, norm_two, inv_two, gains[2])
    grad_middle = grad_top + grad_mid_in
    grad_branch_f, gain_att, bias_att = norm_backward(grad_middle, norm_att, inv_att, gains[1])
    grad_branch = grad_branch_f.astype(low)
    out_left = all_tokens_own(scaled_t.T, me, size)
    out_right = all_tokens(grad_branch, size)

    wide = norm_gain.shape[1]
    squares = jnp.stack(
        [jnp.sum(result * result), jnp.sum(attn_out * attn_out), jnp.sum(ffn_out * ffn_out)]
    )
    norms = jnp.stack([gain_att, gain_two, bias_att, bias_two])
    mids = jnp.stack([mid_gain_grad, mid_bias_grad])
    n_small = 4 + 2 * mid_gain.shape[0] // wide

    def small_rows(s):
        return jnp.concatenate(
            [
                part_of(norms, s, me, size, 1),
                part_of(mids, s, me, size, 1).reshape(-1, wide),
                jnp.pad(squares[None], ((0, 15 - n_small), (0, wide - 3))),
            ],
            axis=0,
        )

    own_rows = fc1_weight.shape[0]

    cut_at = (hidden_width + width) // 2

    def product_a(w):
        return dot(half_of(fc1_left, w, 1), fc1_right[:, :cut_at], 0, 0)

    def product_b(w):
        return jnp.concatenate(
            [
                dot(half_of(fc1_left, w, 1), fc1_right[:, cut_at:], 0, 0),
                dot(half_of(out_left, w, 1), out_right, 0, 0),
            ],
            axis=1,
        )

    sent_a = product_a(1 - bit_of(member, strides[0])).astype(low)
    sent_b = product_b(1 - bit_of(member, strides[-1])).astype(low)

    grad_scaled_t = natural([dot(part, grad_branch, 1, 1) for part in out_parts], me, 0)
    grad_att = (
        grad_scaled_t.reshape(HEADS, HEAD_DIM, rows) * head_scales[:, None, None]
    ).astype(low)
    grad_tiles = lax.all_to_all(grad_att, "ctx", 0, 0, tiled=True, axis_index_groups=head_groups)
    grad_tiles, sent_a, sent_b = lax.optimization_barrier((grad_tiles, sent_a, sent_b))
    orders = (strides, strides[::-1])
    got = [swapped(v, o[0], groups) for v, o in zip((sent_a, sent_b), orders)]
    dq, dk, dv, delta_sum = attend_back(
        info, qs, ks, vs, att, log_total, grad_tiles, low if copies == 1 else f32
    )
    if copies > 1:
        dk, dv = (
            lax.psum_scatter(
                d, "ctx", scatter_dimension=0, tiled=True, axis_index_groups=copy_groups
            ).astype(low)
            for d in (dk, dv)
        )

    grads_out = jnp.stack([dq, dk, dv], axis=1)
    grad_proj_t = lax.all_to_all(
        grads_out, "ctx", 0, 0, tiled=True, axis_index_groups=head_groups
    ).transpose(1, 0, 2, 3).reshape(3 * width, rows)
    head_sums, column_sums = head_grad(gathered, dq, dk, dv)
    my_scale_grad = jnp.sum(delta_sum) / my_scale[0]
    extra = jnp.concatenate(
        [column_sums[0].reshape(3, HEAD_DIM), jnp.full((1, HEAD_DIM), my_scale_grad)], axis=0
    )
    smalls_of = [small_rows(s) for s in range(size)]
    if copies > 1:
        head_sums, extra, smalls_of = (
            lax.psum(d, "ctx", axis_index_groups=copy_groups)
            for d in (head_sums, extra, smalls_of)
        )
    n_head_rows = head_sums.shape[0]
    n_payload = n_head_rows + 32
    extra = jnp.pad(jnp.concatenate([extra, extra], axis=1), ((0, 12), (0, wide - 2 * HEAD_DIM)))

    def with_extra(sums, more, small_sums):
        high = more.astype(low)
        rest_of = (more - high.astype(f32)).astype(low)
        both_parts = high + jnp.roll(rest_of, 4, axis=0)
        return jnp.concatenate([sums.astype(low), both_parts, small_sums.astype(low)], axis=0)

    own_sums = part_of(head_sums, 0, me, size, 1)
    own_extra = extra
    own_small = smalls_of[0]
    for s in range(1, size):
        more_rows = from_member(
            with_extra(part_of(head_sums, size - s, me, size, 1), extra, smalls_of[size - s]),
            s, size,
        ).astype(f32)
        own_sums = own_sums + more_rows[:n_head_rows]
        own_small = own_small + more_rows[n_head_rows + 16 :]
        more_rows = more_rows[n_head_rows : n_head_rows + 16]
        own_extra = own_extra + jnp.pad(more_rows[:4] + more_rows[4:8], ((0, 12), (0, 0)))
    payload = lax.optimization_barrier(with_extra(own_sums, own_extra, own_small))

    got, payload = lax.optimization_barrier((got, payload))
    sums = [
        (product(bit_of(member, o[0])) + g.astype(f32)).astype(low)
        for product, o, g in zip((product_a, product_b), orders, got)
    ]
    for step in range(1, len(strides)):
        bits_now = [bit_of(member, o[step]) for o in orders]
        got = [
            swapped(half_of(v, 1 - bit), o[step], groups)
            for v, bit, o in zip(sums, bits_now, orders)
        ]
        sums = [
            (half_of(v, bit).astype(f32) + g.astype(f32)).astype(low)
            for v, bit, g in zip(sums, bits_now, got)
        ]
    unit = jnp.concatenate(sums, axis=1)
    one_chunk = own_rows // groups
    sent = [
        lax.dynamic_slice_in_dim(unit, (line + k) % lines * one_chunk, one_chunk, 0)
        for k in range(lines)
    ]
    on_lines = [from_line(sent[k], k, plane, groups) for k in range(1, lines)]
    by_permutes = copies == 1
    unit = (sent[0].astype(f32) + sum(g.astype(f32) for g in on_lines)).astype(low)
    got = [from_line(unit, k, plane, groups) for k in range(1, lines)]
    on_line = [payload]
    if by_permutes:
        on_line += [from_line(payload, k, plane, groups) for k in range(1, lines)]
    got, on_line = lax.optimization_barrier((got, on_line))
    near = []
    if by_permutes:
        on_line = jnp.concatenate(on_line, axis=0)
        near = [on_line[:, : wide // 2], on_line[:, wide // 2 :]]
        near = [[v, swapped(v, o[0], groups)] for v, o in zip(near, orders)]
    unit = jnp.concatenate([unit] + got, axis=0)
    parts = [unit[:, :cut_at], unit[:, cut_at:]]
    outward = orders[::-1]
    for step in range(len(strides) - 1):
        got = [swapped(v, o[step], groups) for v, o in zip(parts, outward)]
        got, near = lax.optimization_barrier((got, near))
        parts = [jnp.concatenate([v, g], axis=0) for v, g in zip(parts, got)]
    if by_permutes:
        near = [jnp.concatenate(v, axis=0) for v in near]
        near = [[v, swapped(v, o[1], groups)] for v, o in zip(near, orders)]
    far = [swapped(v, o[-1], groups) for v, o in zip(parts, outward)]

    bits = range(len(strides))
    heads = jnp.arange(HEADS)
    if by_permutes:
        left, right = (
            jnp.concatenate(v, axis=0).reshape(HEADS, n_payload, wide // 2) for v in near
        )
        head_bits = [bit_of(heads, stride) for stride in strides]
        at_l = joined_places(heads // plane, head_bits, bits, member, line, lines, plane)
        at_r = joined_places(heads // plane, head_bits, bits[::-1], member, line, lines, plane)
    else:
        every = lax.all_gather(payload, "ctx", axis=0, axis_index_groups=head_groups)
        left, right = every[:, :, : wide // 2], every[:, :, wide // 2 :]
        at_l = at_r = heads.astype(jnp.int32)
    qkv_sum, gain_parts, bias_parts, scales, small_sums = place_qkv(
        at_l, at_r, left, right, qkv_weight, norm_gain[0].astype(f32), norm_bias[0].astype(f32)
    )
    gain_one, bias_one = jnp.sum(gain_parts, axis=1), jnp.sum(bias_parts, axis=1)
    scale_sum = part_of(scales[:, 0], 0, me, size, 0)
    grad_one = natural([dot(grad_proj_t, part, 0, 1) for part in qkv_parts], me, 1)
    grad_first = norm_backward(grad_one, norm_one, inv_one, gains[0])[0]
    input_grad = (grad_middle + grad_first).astype(low)[None]

    far, qkv_sum, input_grad = lax.optimization_barrier((far, qkv_sum, input_grad))
    block = jnp.arange(groups)
    block_bits = [block // lines // (1 << i) % 2 for i in bits]
    at_a = joined_places(
        block % lines, block_bits[::-1], bits[::-1], member, line, lines, plane
    )
    at_b = joined_places(block % lines, block_bits, bits, member, line, lines, plane)
    ends = [
        [d.reshape(groups // 2, one_chunk, -1) for d in pair] for pair in zip(parts, far)
    ]
    fc1_sum, out_sum = place_sums(at_a, at_b, ends[0], ends[1], hidden_width)
    fc1_sum, fc2_sum = lax.optimization_barrier((fc1_sum, fc2_sum))
    fc1_sum = fc1_sum.reshape(own_rows, hidden_width)
    out_sum = out_sum.reshape(own_rows, width)
    gain_grad = jnp.stack([gain_one, small_sums[0], small_sums[1]])
    bias_grad = jnp.stack([bias_one, small_sums[2], small_sums[3]])
    mid_sums = small_sums[4:n_small].reshape(2, -1)
    mid_gain_sum, mid_bias_sum = mid_sums[0], mid_sums[1]
    rms_values = jnp.sqrt(small_sums[n_small, :3] / (rows * groups * size * width))
    return (
        result.astype(low)[None],
        input_grad,
        qkv_sum,
        out_sum,
        fc1_sum,
        fc2_sum.astype(f32),
        gain_grad,
        bias_grad,
        mid_gain_sum,
        mid_bias_sum,
        scale_sum,
        rms_values,
    )


def solution(mesh):
    split = P("fsdp", "ctx", None)
    by_row = P("fsdp", None)
    by_col = P(None, "fsdp")
    one = P("fsdp")
    return jax.shard_map(
        local,
        mesh=mesh,
        in_specs=(split, split, by_row, by_row, by_row, by_row, by_row, by_col, by_col, one, one, one),
        out_specs=(split, split, by_row, by_row, by_row, by_row, by_col, by_col, one, one, one, P()),
        check_vma=False,
    )
```

```python
from functools import partial

import jax
import jax.numpy as jnp
from jax import lax
from jax.experimental import pallas as pl
from jax.experimental.pallas import tpu as pltpu
from jax.sharding import PartitionSpec as P

HEADS = 16
HEAD_DIM = 64
TILE = 256
EPS = 1e-05
MASKED = -1e30
SCALE = HEAD_DIM ** (-0.5)


def dot(a, b, ca=1, cb=0):
    return lax.dot_general(a, b, (((ca,), (cb,)), ((), ())), preferred_element_type=jnp.float32)


def normalize(values):
    centered = values - jnp.mean(values, axis=-1, keepdims=True)
    inverse = lax.rsqrt(jnp.mean(centered * centered, axis=-1, keepdims=True) + EPS)
    return (centered * inverse, inverse)


def norm_backward(grad_out, normed, inverse, gain_vec):
    grad_normed = grad_out * gain_vec
    grad_in = inverse * (
        grad_normed
        - jnp.mean(grad_normed, axis=-1, keepdims=True)
        - normed * jnp.mean(grad_normed * normed, axis=-1, keepdims=True)
    )
    return (grad_in, jnp.sum(grad_out * normed, axis=0), jnp.sum(grad_out, axis=0))


def sorted_sources(n_tiles):
    return [(t, 0) for t in range(n_tiles)] + [(t, 1) for t in range(n_tiles - 1, -1, -1)]


def pair_up(first, second):
    lane = lax.broadcasted_iota(jnp.int32, first[0].shape, 1)
    left = first[0] if first[1] == 0 else pltpu.roll(first[0], 64, 1)
    right = second[0] if second[1] == 1 else pltpu.roll(second[0], 64, 1)
    return jnp.where(lane < 64, left, right)


def sort_tiles(load, n_tiles, store):
    order = sorted_sources(n_tiles)
    for u in range(n_tiles):
        (ta, ha), (tb, hb) = order[2 * u], order[2 * u + 1]
        store(u, pair_up((load(ta), ha), (load(tb), hb)))


def unsort_tiles(load, n_tiles, store):
    for t in range(n_tiles):
        a, b = t, 2 * n_tiles - 1 - t
        store(t, pair_up((load(a // 2), a % 2), (load(b // 2), b % 2)))


def tile_spans(info_ref, qt, n_q_tiles, half_run, total_blocks):
    group = info_ref[0]
    per_run = n_q_tiles // 2
    low_first = group * half_run
    high_first = total_blocks * 64 - (group + 1) * half_run
    q_first = jnp.where(qt < per_run, low_first + qt * TILE, high_first + (qt - per_run) * TILE)
    start = jnp.int32(0)
    floor_first = jnp.int32(0)
    for d in range(8):
        floor_first = jnp.where(start <= q_first, start, floor_first)
        start = start + info_ref[1 + d]
    return q_first, floor_first // TILE


def query_rows(info_ref, q_first):
    q_pos = q_first + lax.broadcasted_iota(jnp.int32, (1, TILE), 1)
    start = jnp.int32(0)
    floor = jnp.zeros((1, TILE), jnp.int32)
    for d in range(8):
        floor = jnp.where(q_pos >= start, start, floor)
        start = start + info_ref[1 + d]
    return q_pos, floor


def usable_mask(q_pos, floor, kt):
    k_pos = kt * TILE + lax.broadcasted_iota(jnp.int32, (TILE, TILE), 0)
    return (k_pos <= q_pos) & (k_pos >= floor)


def attend_kernel(
    info_ref, hs_ref, q_ref, kv_ref, scaled_ref, att_ref, log_ref, qs_ref, ks_ref, vs_ref, kn_ref,
    *, n_q, n_k, k_at,
):
    per = TILE // 128
    f32 = jnp.float32

    def put(ref):
        def store(u, tile):
            ref[u // per, :, (u % per) * 128 : (u % per) * 128 + 128] = tile.astype(jnp.bfloat16)
        return store

    sort_tiles(lambda t: q_ref[t, 0].astype(f32), n_q, put(qs_ref))
    sort_tiles(lambda t: kv_ref[t, k_at].astype(f32), n_k, put(ks_ref))
    sort_tiles(lambda t: kv_ref[t, k_at + 1].astype(f32), n_k, put(vs_ref))
    for kt in range(n_k // per):
        kn_ref[kt] = ks_ref[kt].astype(f32).T.astype(jnp.bfloat16)

    def one_query_tile(qt, carry):
        q_first, k_low = tile_spans(info_ref, qt, n_q // per, n_q * 64, 2 * n_k)
        q_pos, floor = query_rows(info_ref, q_first)
        q_t = qs_ref[qt]

        def one_key_tile(kt, state):
            high, total, acc = state
            scores = dot(kn_ref[kt], q_t) * SCALE
            usable = usable_mask(q_pos, floor, kt)
            scores = jnp.where(usable, scores, MASKED)
            new_high = jnp.maximum(high, jnp.max(scores, axis=0, keepdims=True))
            probs = jnp.where(usable, jnp.exp(scores - new_high), 0.0)
            fix = jnp.exp(high - new_high)
            total = total * fix + jnp.sum(probs, axis=0, keepdims=True)
            acc = acc * fix + dot(vs_ref[kt], probs.astype(jnp.bfloat16))
            return new_high, total, acc

        high, total, acc = lax.fori_loop(
            k_low,
            q_first // TILE + 1,
            one_key_tile,
            (
                jnp.full((1, TILE), MASKED, f32),
                jnp.zeros((1, TILE), f32),
                jnp.zeros((HEAD_DIM, TILE), f32),
            ),
        )
        att_ref[qt] = acc / total
        log_ref[qt] = high + jnp.log(total)
        return carry

    lax.fori_loop(0, n_q // per, one_query_tile, 0)
    head_scale = hs_ref[0]

    def load(u):
        return att_ref[u // per, :, (u % per) * 128 : (u % per) * 128 + 128]

    def give(t, tile):
        scaled_ref[t] = (tile * head_scale).astype(jnp.bfloat16)

    unsort_tiles(load, n_q, give)


def attend_back_kernel(
    info_ref, qs_ref, ks_ref, vs_ref, att_ref, log_ref, go_ref, dq_ref, dk_ref, dv_ref, dsum_ref,
    go_s, kn_ref, vn_ref, dq_s, dk_s, dv_s,
    *, n_q, n_k,
):
    per = TILE // 128
    f32 = jnp.float32
    low = jnp.bfloat16

    def store(u, tile):
        go_s[u // per, :, (u % per) * 128 : (u % per) * 128 + 128] = tile.astype(low)

    sort_tiles(lambda t: go_ref[t].astype(f32), n_q, store)
    for kt in range(n_k // per):
        kn_ref[kt] = ks_ref[kt].astype(f32).T.astype(low)
        vn_ref[kt] = vs_ref[kt].astype(f32).T.astype(low)
        dk_s[kt] = jnp.zeros((TILE, HEAD_DIM), f32)
        dv_s[kt] = jnp.zeros((TILE, HEAD_DIM), f32)
    dsum_ref[...] = jnp.zeros((1, TILE), f32)

    def one_query_tile(qt, carry):
        q_first, k_low = tile_spans(info_ref, qt, n_q // per, n_q * 64, 2 * n_k)
        q_pos, floor = query_rows(info_ref, q_first)
        q_t = qs_ref[qt]
        g_t = go_s[qt]
        q_n = q_t.astype(f32).T.astype(low)
        g_n = g_t.astype(f32).T.astype(low)
        log_total = log_ref[qt]
        delta = jnp.sum(g_t.astype(f32) * att_ref[qt], axis=0, keepdims=True)
        dsum_ref[...] += delta

        def one_key_tile(kt, acc):
            scores = dot(kn_ref[kt], q_t) * SCALE
            usable = usable_mask(q_pos, floor, kt)
            probs = jnp.where(usable, jnp.exp(scores - log_total), 0.0)
            grad_probs = dot(vn_ref[kt], g_t)
            grad_scores = (probs * (grad_probs - delta)).astype(low)
            dv_s[kt] += dot(probs.astype(low), g_n)
            dk_s[kt] += dot(grad_scores, q_n)
            return acc + dot(ks_ref[kt], grad_scores)

        dq_s[qt] = lax.fori_loop(
            k_low, q_first // TILE + 1, one_key_tile, jnp.zeros((HEAD_DIM, TILE), f32)
        )
        return carry

    lax.fori_loop(0, n_q // per, one_query_tile, 0)

    def load_q(u):
        return dq_s[u // per, :, (u % per) * 128 : (u % per) * 128 + 128]

    def give_q(t, tile):
        dq_ref[t] = (tile * SCALE).astype(dq_ref.dtype)

    def load_k(u):
        return dk_s[u // per, (u % per) * 128 : (u % per) * 128 + 128, :].T

    def give_k(t, tile):
        dk_ref[t] = (tile * SCALE).astype(dk_ref.dtype)

    def load_v(u):
        return dv_s[u // per, (u % per) * 128 : (u % per) * 128 + 128, :].T

    def give_v(t, tile):
        dv_ref[t] = tile.astype(dv_ref.dtype)

    unsort_tiles(load_q, n_q, give_q)
    unsort_tiles(load_k, n_k, give_k)
    unsort_tiles(load_v, n_k, give_v)


def head_grad_kernel(x_ref, dq_ref, dk_ref, dv_ref, m_ref, c_ref):
    low, f32 = jnp.bfloat16, jnp.float32

    @pl.when(pl.program_id(0) == 0)
    def _():
        m_ref[...] = jnp.zeros(m_ref.shape, f32)
        c_ref[...] = jnp.zeros(c_ref.shape, f32)

    x = jnp.concatenate([x_ref[0], x_ref[1]], axis=0).astype(f32)
    normed = normalize(x)[0].astype(low)
    grads = jnp.concatenate(
        [jnp.concatenate([ref[0], ref[1]], axis=1) for ref in (dq_ref, dk_ref, dv_ref)], axis=0
    )
    m_ref[...] += dot(grads, normed)
    c_ref[...] += dot(jnp.ones((8, grads.shape[1]), low), grads, 1, 1)


def takes(microseconds):
    return pl.CostEstimate(
        flops=0, transcendentals=0, bytes_accessed=int(microseconds * 3.2e6)
    )


def on_chip(n):
    return [pl.BlockSpec(memory_space=pltpu.VMEM)] * n


def in_scalars(n):
    return [pl.BlockSpec(memory_space=pltpu.SMEM)] * n


def attend(info, head_scale, q_tiles, kv_tiles, k_at):
    n_q, n_k = q_tiles.shape[0], kv_tiles.shape[0]
    nq, nk = n_q * 128 // TILE, n_k * 128 // TILE
    low, f32 = jnp.bfloat16, jnp.float32
    return pl.pallas_call(
        partial(attend_kernel, n_q=n_q, n_k=n_k, k_at=k_at),
        in_specs=in_scalars(2) + on_chip(2),
        out_specs=tuple(on_chip(6)),
        out_shape=(
            jax.ShapeDtypeStruct((n_q, HEAD_DIM, 128), low),
            jax.ShapeDtypeStruct((nq, HEAD_DIM, TILE), f32),
            jax.ShapeDtypeStruct((nq, 1, TILE), f32),
            jax.ShapeDtypeStruct((nq, HEAD_DIM, TILE), low),
            jax.ShapeDtypeStruct((nk, HEAD_DIM, TILE), low),
            jax.ShapeDtypeStruct((nk, HEAD_DIM, TILE), low),
        ),
        scratch_shapes=[pltpu.VMEM((nk, TILE, HEAD_DIM), low)],
        compiler_params=pltpu.CompilerParams(vmem_limit_bytes=48 << 20),
        cost_estimate=takes(10),
        name="attend",
    )(info, head_scale, q_tiles, kv_tiles)


def attend_back(info, qs, ks, vs, att, log_total, grad_tiles, kv_type):
    n_q = grad_tiles.shape[0]
    nq, nk = qs.shape[0], ks.shape[0]
    n_k = nk * TILE // 128
    low, f32 = jnp.bfloat16, jnp.float32
    return pl.pallas_call(
        partial(attend_back_kernel, n_q=n_q, n_k=n_k),
        in_specs=in_scalars(1) + on_chip(6),
        out_specs=tuple(on_chip(4)),
        out_shape=(
            jax.ShapeDtypeStruct((n_q, HEAD_DIM, 128), low),
            jax.ShapeDtypeStruct((n_k, HEAD_DIM, 128), kv_type),
            jax.ShapeDtypeStruct((n_k, HEAD_DIM, 128), kv_type),
            jax.ShapeDtypeStruct((1, TILE), f32),
        ),
        scratch_shapes=[
            pltpu.VMEM((nq, HEAD_DIM, TILE), low),
            pltpu.VMEM((nk, TILE, HEAD_DIM), low),
            pltpu.VMEM((nk, TILE, HEAD_DIM), low),
            pltpu.VMEM((nq, HEAD_DIM, TILE), f32),
            pltpu.VMEM((nk, TILE, HEAD_DIM), f32),
            pltpu.VMEM((nk, TILE, HEAD_DIM), f32),
        ],
        compiler_params=pltpu.CompilerParams(vmem_limit_bytes=48 << 20),
        cost_estimate=takes(10),
        name="attend_back",
    )(info, qs, ks, vs, att, log_total, grad_tiles)


def stream_tiles(gathered, which):
    _, _, rows, width = gathered.shape
    return pl.BlockSpec((2, pl.Squeezed(), rows, width), lambda i: (i, which, 0, 0))


def head_grad(gathered, dq, dk, dv):
    width = gathered.shape[3]
    f32 = jnp.float32
    tiles = pl.BlockSpec((2, HEAD_DIM, 128), lambda i: (i, 0, 0))
    return pl.pallas_call(
        head_grad_kernel,
        grid=(gathered.shape[0] // 2,),
        in_specs=[stream_tiles(gathered, 0)] + [tiles] * 3,
        out_specs=(
            pl.BlockSpec((3 * HEAD_DIM, width), lambda i: (0, 0)),
            pl.BlockSpec((8, 3 * HEAD_DIM), lambda i: (0, 0)),
        ),
        out_shape=(
            jax.ShapeDtypeStruct((3 * HEAD_DIM, width), f32),
            jax.ShapeDtypeStruct((8, 3 * HEAD_DIM), f32),
        ),
        cost_estimate=takes(8),
        name="head_grad",
    )(gathered, dq, dk, dv)


def place_sums_kernel(
    at_a_ref, at_b_ref, a_near_ref, a_far_ref, b_near_ref, b_far_ref, fc1_ref, out_ref
):
    f32 = jnp.float32
    per, n, hidden_width = fc1_ref.shape
    half = a_near_ref.shape[0]
    cut_at = a_near_ref.shape[2]
    rest = hidden_width - cut_at

    def put_a(i, ref, at):
        fc1_ref[i, :, :cut_at] = ref[at].astype(f32)

    def put_b(i, ref, at):
        fc1_ref[i, :, cut_at:] = ref[at, :, :rest].astype(f32)
        out_ref[i] = ref[at, :, rest:].astype(f32)

    for i in range(per):
        r = pl.program_id(0) * per + i
        for put, at, near, far in (
            (put_a, at_a_ref[r], a_near_ref, a_far_ref),
            (put_b, at_b_ref[r], b_near_ref, b_far_ref),
        ):
            pl.when(at < half)(partial(put, i, near, at))
            pl.when(at >= half)(partial(put, i, far, at - half))


def place_sums(at_a, at_b, sums_a, sums_b, hidden_width):
    half, n, wide_a = sums_a[0].shape
    wide_b = sums_b[0].shape[2]
    blocks = 2 * half
    per = 2
    width = wide_a + wide_b - hidden_width
    f32 = jnp.float32

    def out_block(w):
        return pl.BlockSpec((per, n, w), lambda r, at_a_ref, at_b_ref: (r, 0, 0))

    return pl.pallas_call(
        place_sums_kernel,
        grid_spec=pltpu.PrefetchScalarGridSpec(
            num_scalar_prefetch=2,
            grid=(blocks // per,),
            in_specs=on_chip(4),
            out_specs=(out_block(hidden_width), out_block(width)),
        ),
        out_shape=(
            jax.ShapeDtypeStruct((blocks, n, hidden_width), f32),
            jax.ShapeDtypeStruct((blocks, n, width), f32),
        ),
        compiler_params=pltpu.CompilerParams(vmem_limit_bytes=48 << 20),
        cost_estimate=takes(7),
        name="place_sums",
    )(at_a, at_b, *sums_a, *sums_b)


def place_qkv_kernel(
    at_l_ref, at_r_ref, left_ref, right_ref, weight_ref, gain_ref, bias_ref,
    grad_ref, gain_sum_ref, bias_sum_ref, scale_ref, small_ref,
):
    f32 = jnp.float32
    step = pl.program_id(0)
    n_rows = 3 * HEAD_DIM
    half = left_ref.shape[2]
    pairs = grad_ref.shape[1] // 128
    per = HEADS // 2 // pairs
    which = step // per
    row = lax.broadcasted_iota(jnp.int32, (16, 128), 0)
    lane = lax.broadcasted_iota(jnp.int32, (1, 128), 1)

    def extra_row(head, i):
        rows = left_ref[at_l_ref[head], n_rows : n_rows + 16, :128].astype(f32)
        return jnp.sum(jnp.where((row == i) | (row == i + 4), rows, 0.0), axis=0, keepdims=True)

    @pl.when(step == 0)
    def _():
        gain_sum_ref[...] = jnp.zeros(gain_sum_ref.shape, f32)
        bias_sum_ref[...] = jnp.zeros(bias_sum_ref.shape, f32)
        for side, ref in enumerate((left_ref, right_ref)):
            small_ref[:, side * half : side * half + half] = sum(
                ref[head, n_rows + 16 :, :].astype(f32) for head in range(HEADS)
            )
        for head in range(HEADS):
            scale_ref[head : head + 1, :] = extra_row(head, 3)

    rows = pl.ds(pl.multiple_of(which * HEAD_DIM, HEAD_DIM), HEAD_DIM)
    for pair in range(pairs):
        first = 2 * (step % per * pairs + pair)
        j = slice(pair * 128, pair * 128 + 128)
        columns = jnp.where(lane < HEAD_DIM, extra_row(first, which), extra_row(first + 1, which))
        for side, (ref, at_ref) in enumerate(((left_ref, at_l_ref), (right_ref, at_r_ref))):
            sums = jnp.concatenate(
                [ref[at_ref[first], rows, :], ref[at_ref[first + 1], rows, :]], axis=0
            ).astype(f32).T
            d = slice(side * half, side * half + half)
            weight = weight_ref[d, j].astype(f32)
            grad_ref[d, j] = sums * gain_ref[d, :] + bias_ref[d, :] * columns
            gain_sum_ref[d, :] += weight * sums
            bias_sum_ref[d, :] += weight * columns


def place_qkv(at_l, at_r, left, right, weight, gain, bias):
    wide, n_columns = weight.shape
    f32 = jnp.float32
    step = 512

    def whole(shape):
        return pl.BlockSpec(shape, lambda i, at_l_ref, at_r_ref: (0,) * len(shape))

    column = pl.BlockSpec((wide, step), lambda i, at_l_ref, at_r_ref: (0, i))
    outs = ((wide, 128), (wide, 128), (HEADS, 128), (16, wide))
    return pl.pallas_call(
        place_qkv_kernel,
        grid_spec=pltpu.PrefetchScalarGridSpec(
            num_scalar_prefetch=2,
            grid=(n_columns // step,),
            in_specs=[
                whole(left.shape), whole(right.shape), column, whole((wide, 1)), whole((wide, 1)),
            ],
            out_specs=(column,) + tuple(whole(shape) for shape in outs),
        ),
        out_shape=(jax.ShapeDtypeStruct((wide, n_columns), f32),)
        + tuple(jax.ShapeDtypeStruct(shape, f32) for shape in outs),
        compiler_params=pltpu.CompilerParams(vmem_limit_bytes=48 << 20),
        cost_estimate=takes(9),
        name="place_qkv",
    )(at_l, at_r, left, right, weight, gain[:, None], bias[:, None])


def from_member(value, s, size):
    return lax.ppermute(value, "fsdp", [((i + s) % size, i) for i in range(size)])


def gather_parts(shard, size):
    return [shard] + [from_member(shard, s, size) for s in range(1, size)]


def part_of(value, s, me, size, axis):
    width = value.shape[axis] // size
    return lax.dynamic_slice_in_dim(value, ((me + s) % size) * width, width, axis)


def natural(parts, me, axis):
    size = len(parts)
    twice = jnp.concatenate(parts + parts, axis=axis)
    width = parts[0].shape[axis]
    return lax.dynamic_slice_in_dim(twice, ((size - me) % size) * width, size * width, axis)


def times_parts(value, parts, me):
    size = len(parts)
    total = dot(part_of(value, 0, me, size, 1), parts[0])
    for s in range(1, size):
        total = total + dot(part_of(value, s, me, size, 1), parts[s])
    return total


def all_tokens(value, size):
    return jnp.concatenate([value] + [from_member(value, s, size) for s in range(1, size)], axis=0)


def all_tokens_own(value, me, size):
    pieces = [part_of(value, 0, me, size, 1)]
    for s in range(1, size):
        pieces.append(from_member(part_of(value, size - s, me, size, 1), s, size))
    return jnp.concatenate(pieces, axis=0)


def swapped(value, stride, groups):
    return lax.ppermute(value, "ctx", [(i, i ^ stride) for i in range(groups)])


def half_of(value, which, axis=0):
    n = value.shape[axis] // 2
    return lax.dynamic_slice_in_dim(value, which * n, n, axis)


def bit_of(member, stride):
    return (member // stride) % 2


def from_line(value, k, plane, groups):
    return lax.ppermute(value, "ctx", [(i, (i + k * plane) % groups) for i in range(groups)])


def joined_places(lines_of, bits_of, order, member, line, lines, plane):
    place = (line - lines_of) % lines
    step = lines
    for i in order:
        place = place + (bits_of[i] ^ bit_of(member, 1 << i)) * step
        step = 2 * step
    return place.astype(jnp.int32)


def local(
    inputs, cotangent, doc_lengths, qkv_weight, out_weight, fc1_weight, fc2_weight,
    norm_gain, norm_bias, mid_gain, mid_bias, head_scale,
):
    low, f32 = jnp.bfloat16, jnp.float32
    groups = lax.axis_size("ctx")
    size = lax.axis_size("fsdp")
    member = lax.axis_index("ctx")
    me = lax.axis_index("fsdp")
    x_low = inputs[0]
    rows, width = x_low.shape
    hidden_width = fc1_weight.shape[1]
    copies = groups // HEADS
    head_groups = [[g * HEADS + i for i in range(HEADS)] for g in range(copies)]
    copy_groups = [[g * HEADS + i for g in range(copies)] for i in range(HEADS)]
    head = member % HEADS
    lines = 1
    while lines * lines < groups:
        lines = 2 * lines
    plane = groups // lines
    line = member // plane
    strides = [1 << i for i in range(plane.bit_length() - 1)]
    info = jnp.concatenate([(member // HEADS)[None].astype(jnp.int32), doc_lengths[0]])

    gathered = lax.all_gather(
        x_low[None],
        "ctx", axis=0, axis_index_groups=None if copies == 1 else head_groups,
    )
    norm_vecs = jnp.concatenate([norm_gain, norm_bias], axis=0)
    norm_vecs = natural(gather_parts(norm_vecs, size), me, 1).astype(f32)
    norm_vecs, qkv_shard = lax.optimization_barrier((norm_vecs, qkv_weight))
    gains, biases = norm_vecs[:3], norm_vecs[3:]
    qkv_parts = gather_parts(qkv_shard, size)

    x_local = x_low.astype(f32)
    norm_one, inv_one = normalize(x_local)
    normed_one = (norm_one * gains[0] + biases[0]).astype(low)
    normed_one, small, out_shard, fc1_shard, fc2_shard = lax.optimization_barrier(
        (
            normed_one, jnp.concatenate([mid_gain, mid_bias, head_scale]),
            out_weight, fc1_weight, fc2_weight,
        )
    )
    smalls = gather_parts(small, size)
    out_parts = gather_parts(out_shard, size)
    fc1_parts = gather_parts(fc1_shard, size)
    fc2_parts = gather_parts(fc2_shard, size)
    n_mid = mid_gain.size
    cut = [0, n_mid, 2 * n_mid, small.size]
    mid_gains, mid_biases, head_scales = (
        natural([v[cut[i] : cut[i + 1]] for v in smalls], me, 0).astype(f32) for i in range(3)
    )
    my_scale = lax.dynamic_slice_in_dim(head_scales, head, 1, 0)
    project_t = sum(
        dot(qkv_parts[s], part_of(normed_one, s, me, size, 1), 0, 1) for s in range(size)
    ).astype(low)
    by_head = project_t.reshape(3, HEADS, HEAD_DIM, rows).transpose(1, 0, 2, 3)
    qkv_tiles = lax.all_to_all(by_head, "ctx", 0, 0, tiled=True, axis_index_groups=head_groups)
    if copies == 1:
        kv_tiles, k_at = qkv_tiles, 1
    else:
        kv_tiles, k_at = lax.all_gather(
            qkv_tiles[:, 1:], "ctx", axis=0, tiled=True, axis_index_groups=copy_groups
        ), 0
    scaled_tiles, att, log_total, qs, ks, vs = attend(info, my_scale, qkv_tiles, kv_tiles, k_at)
    scaled_t = lax.all_to_all(
        scaled_tiles, "ctx", 0, 0, tiled=True, axis_index_groups=head_groups
    ).reshape(width, rows)
    branch = sum(dot(part_of(scaled_t, s, me, size, 0), out_parts[s], 0, 0) for s in range(size))
    norm_att, inv_att = normalize(branch)
    attn_out = norm_att * gains[1] + biases[1]
    middle = x_local + attn_out
    norm_two, inv_two = normalize(middle)
    normed_two = (norm_two * gains[2] + biases[2]).astype(low)
    hidden = times_parts(normed_two, fc1_parts, me)
    active, gelu_back = jax.vjp(partial(jax.nn.gelu, approximate=True), hidden)
    norm_mid, inv_mid = normalize(active)
    mixed_in = (norm_mid * mid_gains + mid_biases).astype(low)
    ffn_out = times_parts(mixed_in, fc2_parts, me)
    result = middle + ffn_out

    grad_ffn = cotangent[0]
    grad_top = grad_ffn.astype(f32)
    fc2_grad = dot(
        all_tokens_own(mixed_in, me, size), all_tokens(grad_ffn, size), 0, 0
    ).astype(low)
    fc2_grad, norm_mid = lax.optimization_barrier((fc2_grad, norm_mid))
    fc2_sum = lax.psum(fc2_grad, "ctx")
    grad_mixed = natural([dot(grad_ffn, part, 1, 1) for part in fc2_parts], me, 1)
    grad_active, mid_gain_grad, mid_bias_grad = norm_backward(
        grad_mixed, norm_mid, inv_mid, mid_gains
    )
    grad_hidden = gelu_back(grad_active)[0].astype(low)
    fc1_left = all_tokens_own(normed_two, me, size)
    fc1_right = all_tokens(grad_hidden, size)
    grad_two = natural([dot(grad_hidden, part, 1, 1) for part in fc1_parts], me, 1)
    grad_mid_in, gain_two, bias_two = norm_backward(grad_two, norm_two, inv_two, gains[2])
    grad_middle = grad_top + grad_mid_in
    grad_branch_f, gain_att, bias_att = norm_backward(grad_middle, norm_att, inv_att, gains[1])
    grad_branch = grad_branch_f.astype(low)
    out_left = all_tokens_own(scaled_t.T, me, size)
    out_right = all_tokens(grad_branch, size)

    wide = norm_gain.shape[1]
    squares = jnp.stack(
        [jnp.sum(result * result), jnp.sum(attn_out * attn_out), jnp.sum(ffn_out * ffn_out)]
    )
    norms = jnp.stack([gain_att, gain_two, bias_att, bias_two])
    mids = jnp.stack([mid_gain_grad, mid_bias_grad])
    n_small = 4 + 2 * mid_gain.shape[0] // wide

    def small_rows(s):
        return jnp.concatenate(
            [
                part_of(norms, s, me, size, 1),
                part_of(mids, s, me, size, 1).reshape(-1, wide),
                jnp.pad(squares[None], ((0, 15 - n_small), (0, wide - 3))),
            ],
            axis=0,
        )

    own_rows = fc1_weight.shape[0]

    cut_at = (hidden_width + width) // 2

    def product_a(w):
        return dot(half_of(fc1_left, w, 1), fc1_right[:, :cut_at], 0, 0)

    def product_b(w):
        return jnp.concatenate(
            [
                dot(half_of(fc1_left, w, 1), fc1_right[:, cut_at:], 0, 0),
                dot(half_of(out_left, w, 1), out_right, 0, 0),
            ],
            axis=1,
        )

    sent_a = product_a(1 - bit_of(member, strides[0])).astype(low)
    sent_b = product_b(1 - bit_of(member, strides[-1])).astype(low)

    grad_scaled_t = natural([dot(part, grad_branch, 1, 1) for part in out_parts], me, 0)
    grad_att = (
        grad_scaled_t.reshape(HEADS, HEAD_DIM, rows) * head_scales[:, None, None]
    ).astype(low)
    grad_tiles = lax.all_to_all(grad_att, "ctx", 0, 0, tiled=True, axis_index_groups=head_groups)
    grad_tiles, sent_a, sent_b = lax.optimization_barrier((grad_tiles, sent_a, sent_b))
    orders = (strides, strides[::-1])
    got = [swapped(v, o[0], groups) for v, o in zip((sent_a, sent_b), orders)]
    dq, dk, dv, delta_sum = attend_back(
        info, qs, ks, vs, att, log_total, grad_tiles, low if copies == 1 else f32
    )
    if copies > 1:
        dk, dv = (
            lax.psum_scatter(
                d, "ctx", scatter_dimension=0, tiled=True, axis_index_groups=copy_groups
            ).astype(low)
            for d in (dk, dv)
        )

    grads_out = jnp.stack([dq, dk, dv], axis=1)
    grad_proj_t = lax.all_to_all(
        grads_out, "ctx", 0, 0, tiled=True, axis_index_groups=head_groups
    ).transpose(1, 0, 2, 3).reshape(3 * width, rows)
    head_sums, column_sums = head_grad(gathered, dq, dk, dv)
    my_scale_grad = jnp.sum(delta_sum) / my_scale[0]
    extra = jnp.concatenate(
        [column_sums[0].reshape(3, HEAD_DIM), jnp.full((1, HEAD_DIM), my_scale_grad)], axis=0
    )
    smalls_of = [small_rows(s) for s in range(size)]
    if copies > 1:
        head_sums, extra, smalls_of = (
            lax.psum(d, "ctx", axis_index_groups=copy_groups)
            for d in (head_sums, extra, smalls_of)
        )
    n_head_rows = head_sums.shape[0]
    n_payload = n_head_rows + 32
    extra = jnp.pad(jnp.concatenate([extra, extra], axis=1), ((0, 12), (0, wide - 2 * HEAD_DIM)))

    def with_extra(sums, more, small_sums):
        high = more.astype(low)
        rest_of = (more - high.astype(f32)).astype(low)
        both_parts = high + jnp.roll(rest_of, 4, axis=0)
        return jnp.concatenate([sums.astype(low), both_parts, small_sums.astype(low)], axis=0)

    own_sums = part_of(head_sums, 0, me, size, 1)
    own_extra = extra
    own_small = smalls_of[0]
    for s in range(1, size):
        more_rows = from_member(
            with_extra(part_of(head_sums, size - s, me, size, 1), extra, smalls_of[size - s]),
            s, size,
        ).astype(f32)
        own_sums = own_sums + more_rows[:n_head_rows]
        own_small = own_small + more_rows[n_head_rows + 16 :]
        more_rows = more_rows[n_head_rows : n_head_rows + 16]
        own_extra = own_extra + jnp.pad(more_rows[:4] + more_rows[4:8], ((0, 12), (0, 0)))
    payload = lax.optimization_barrier(with_extra(own_sums, own_extra, own_small))

    got, payload = lax.optimization_barrier((got, payload))
    sums = [
        (product(bit_of(member, o[0])) + g.astype(f32)).astype(low)
        for product, o, g in zip((product_a, product_b), orders, got)
    ]
    for step in range(1, len(strides)):
        bits_now = [bit_of(member, o[step]) for o in orders]
        got = [
            swapped(half_of(v, 1 - bit), o[step], groups)
            for v, bit, o in zip(sums, bits_now, orders)
        ]
        sums = [
            (half_of(v, bit).astype(f32) + g.astype(f32)).astype(low)
            for v, bit, g in zip(sums, bits_now, got)
        ]
    unit = jnp.concatenate(sums, axis=1)
    one_chunk = own_rows // groups
    sent = [
        lax.dynamic_slice_in_dim(unit, (line + k) % lines * one_chunk, one_chunk, 0)
        for k in range(lines)
    ]
    on_lines = [from_line(sent[k], k, plane, groups) for k in range(1, lines)]
    by_permutes = copies == 1
    unit = (sent[0].astype(f32) + sum(g.astype(f32) for g in on_lines)).astype(low)
    got = [from_line(unit, k, plane, groups) for k in range(1, lines)]
    on_line = [payload]
    if by_permutes:
        on_line += [from_line(payload, k, plane, groups) for k in range(1, lines)]
    got, on_line = lax.optimization_barrier((got, on_line))
    near = []
    if by_permutes:
        on_line = jnp.concatenate(on_line, axis=0)
        near = [on_line[:, : wide // 2], on_line[:, wide // 2 :]]
        near = [[v, swapped(v, o[0], groups)] for v, o in zip(near, orders)]
    unit = jnp.concatenate([unit] + got, axis=0)
    parts = [unit[:, :cut_at], unit[:, cut_at:]]
    outward = orders[::-1]
    for step in range(len(strides) - 1):
        got = [swapped(v, o[step], groups) for v, o in zip(parts, outward)]
        got, near = lax.optimization_barrier((got, near))
        parts = [jnp.concatenate([v, g], axis=0) for v, g in zip(parts, got)]
    if by_permutes:
        near = [jnp.concatenate(v, axis=0) for v in near]
        near = [[v, swapped(v, o[1], groups)] for v, o in zip(near, orders)]
    far = [swapped(v, o[-1], groups) for v, o in zip(parts, outward)]

    bits = range(len(strides))
    heads = jnp.arange(HEADS)
    if by_permutes:
        left, right = (
            jnp.concatenate(v, axis=0).reshape(HEADS, n_payload, wide // 2) for v in near
        )
        head_bits = [bit_of(heads, stride) for stride in strides]
        at_l = joined_places(heads // plane, head_bits, bits, member, line, lines, plane)
        at_r = joined_places(heads // plane, head_bits, bits[::-1], member, line, lines, plane)
    else:
        every = lax.all_gather(payload, "ctx", axis=0, axis_index_groups=head_groups)
        left, right = every[:, :, : wide // 2], every[:, :, wide // 2 :]
        at_l = at_r = heads.astype(jnp.int32)
    qkv_sum, gain_parts, bias_parts, scales, small_sums = place_qkv(
        at_l, at_r, left, right, qkv_weight, norm_gain[0].astype(f32), norm_bias[0].astype(f32)
    )
    gain_one, bias_one = jnp.sum(gain_parts, axis=1), jnp.sum(bias_parts, axis=1)
    scale_sum = part_of(scales[:, 0], 0, me, size, 0)
    grad_one = natural([dot(grad_proj_t, part, 0, 1) for part in qkv_parts], me, 1)
    grad_first = norm_backward(grad_one, norm_one, inv_one, gains[0])[0]
    input_grad = (grad_middle + grad_first).astype(low)[None]

    fc2_sum, qkv_sum = lax.optimization_barrier((fc2_sum, qkv_sum))
    fc2_sum = fc2_sum.astype(f32)
    far, fc2_sum = lax.optimization_barrier((far, fc2_sum))
    far, qkv_sum, input_grad = lax.optimization_barrier((far, qkv_sum, input_grad))
    block = jnp.arange(groups)
    block_bits = [block // lines // (1 << i) % 2 for i in bits]
    at_a = joined_places(
        block % lines, block_bits[::-1], bits[::-1], member, line, lines, plane
    )
    at_b = joined_places(block % lines, block_bits, bits, member, line, lines, plane)
    ends = [
        [d.reshape(groups // 2, one_chunk, -1) for d in pair] for pair in zip(parts, far)
    ]
    fc1_sum, out_sum = place_sums(at_a, at_b, ends[0], ends[1], hidden_width)
    fc1_sum = fc1_sum.reshape(own_rows, hidden_width)
    out_sum = out_sum.reshape(own_rows, width)
    gain_grad = jnp.stack([gain_one, small_sums[0], small_sums[1]])
    bias_grad = jnp.stack([bias_one, small_sums[2], small_sums[3]])
    mid_sums = small_sums[4:n_small].reshape(2, -1)
    mid_gain_sum, mid_bias_sum = mid_sums[0], mid_sums[1]
    rms_values = jnp.sqrt(small_sums[n_small, :3] / (rows * groups * size * width))
    return (
        result.astype(low)[None],
        input_grad,
        qkv_sum,
        out_sum,
        fc1_sum,
        fc2_sum,
        gain_grad,
        bias_grad,
        mid_gain_sum,
        mid_bias_sum,
        scale_sum,
        rms_values,
    )


def solution(mesh):
    split = P("fsdp", "ctx", None)
    by_row = P("fsdp", None)
    by_col = P(None, "fsdp")
    one = P("fsdp")
    return jax.shard_map(
        local,
        mesh=mesh,
        in_specs=(split, split, by_row, by_row, by_row, by_row, by_row, by_col, by_col, one, one, one),
        out_specs=(split, split, by_row, by_row, by_row, by_row, by_col, by_col, one, one, one, P()),
        check_vma=False,
    )
```

```python
from functools import partial

import jax
import jax.numpy as jnp
from jax import lax
from jax.experimental import pallas as pl
from jax.experimental.pallas import tpu as pltpu
from jax.sharding import PartitionSpec as P

HEADS = 16
HEAD_DIM = 64
TILE = 256
EPS = 1e-05
MASKED = -1e30
SCALE = HEAD_DIM ** (-0.5)


def dot(a, b, ca=1, cb=0):
    return lax.dot_general(a, b, (((ca,), (cb,)), ((), ())), preferred_element_type=jnp.float32)


def normalize(values):
    centered = values - jnp.mean(values, axis=-1, keepdims=True)
    inverse = lax.rsqrt(jnp.mean(centered * centered, axis=-1, keepdims=True) + EPS)
    return (centered * inverse, inverse)


def norm_backward(grad_out, normed, inverse, gain_vec):
    grad_normed = grad_out * gain_vec
    grad_in = inverse * (
        grad_normed
        - jnp.mean(grad_normed, axis=-1, keepdims=True)
        - normed * jnp.mean(grad_normed * normed, axis=-1, keepdims=True)
    )
    return (grad_in, jnp.sum(grad_out * normed, axis=0), jnp.sum(grad_out, axis=0))


def sorted_sources(n_tiles):
    return [(t, 0) for t in range(n_tiles)] + [(t, 1) for t in range(n_tiles - 1, -1, -1)]


def pair_up(first, second):
    lane = lax.broadcasted_iota(jnp.int32, first[0].shape, 1)
    left = first[0] if first[1] == 0 else pltpu.roll(first[0], 64, 1)
    right = second[0] if second[1] == 1 else pltpu.roll(second[0], 64, 1)
    return jnp.where(lane < 64, left, right)


def sort_tiles(load, n_tiles, store):
    order = sorted_sources(n_tiles)
    for u in range(n_tiles):
        (ta, ha), (tb, hb) = order[2 * u], order[2 * u + 1]
        store(u, pair_up((load(ta), ha), (load(tb), hb)))


def unsort_tiles(load, n_tiles, store):
    for t in range(n_tiles):
        a, b = t, 2 * n_tiles - 1 - t
        store(t, pair_up((load(a // 2), a % 2), (load(b // 2), b % 2)))


def tile_spans(info_ref, qt, n_q_tiles, half_run, total_blocks):
    group = info_ref[0]
    per_run = n_q_tiles // 2
    low_first = group * half_run
    high_first = total_blocks * 64 - (group + 1) * half_run
    q_first = jnp.where(qt < per_run, low_first + qt * TILE, high_first + (qt - per_run) * TILE)
    start = jnp.int32(0)
    floor_first = jnp.int32(0)
    for d in range(8):
        floor_first = jnp.where(start <= q_first, start, floor_first)
        start = start + info_ref[1 + d]
    return q_first, floor_first // TILE


def query_rows(info_ref, q_first):
    q_pos = q_first + lax.broadcasted_iota(jnp.int32, (1, TILE), 1)
    start = jnp.int32(0)
    floor = jnp.zeros((1, TILE), jnp.int32)
    for d in range(8):
        floor = jnp.where(q_pos >= start, start, floor)
        start = start + info_ref[1 + d]
    return q_pos, floor


def usable_mask(q_pos, floor, kt):
    k_pos = kt * TILE + lax.broadcasted_iota(jnp.int32, (TILE, TILE), 0)
    return (k_pos <= q_pos) & (k_pos >= floor)


def attend_kernel(
    info_ref, hs_ref, q_ref, kv_ref, scaled_ref, att_ref, log_ref, qs_ref, ks_ref, vs_ref, kn_ref,
    *, n_q, n_k, k_at,
):
    per = TILE // 128
    f32 = jnp.float32

    def put(ref):
        def store(u, tile):
            ref[u // per, :, (u % per) * 128 : (u % per) * 128 + 128] = tile.astype(jnp.bfloat16)
        return store

    sort_tiles(lambda t: q_ref[t, 0].astype(f32), n_q, put(qs_ref))
    sort_tiles(lambda t: kv_ref[t, k_at].astype(f32), n_k, put(ks_ref))
    sort_tiles(lambda t: kv_ref[t, k_at + 1].astype(f32), n_k, put(vs_ref))
    for kt in range(n_k // per):
        kn_ref[kt] = ks_ref[kt].astype(f32).T.astype(jnp.bfloat16)

    def one_query_tile(qt, carry):
        q_first, k_low = tile_spans(info_ref, qt, n_q // per, n_q * 64, 2 * n_k)
        q_pos, floor = query_rows(info_ref, q_first)
        q_t = qs_ref[qt]

        def one_key_tile(kt, state):
            high, total, acc = state
            scores = dot(kn_ref[kt], q_t) * SCALE
            usable = usable_mask(q_pos, floor, kt)
            scores = jnp.where(usable, scores, MASKED)
            new_high = jnp.maximum(high, jnp.max(scores, axis=0, keepdims=True))
            probs = jnp.where(usable, jnp.exp(scores - new_high), 0.0)
            fix = jnp.exp(high - new_high)
            total = total * fix + jnp.sum(probs, axis=0, keepdims=True)
            acc = acc * fix + dot(vs_ref[kt], probs.astype(jnp.bfloat16))
            return new_high, total, acc

        high, total, acc = lax.fori_loop(
            k_low,
            q_first // TILE + 1,
            one_key_tile,
            (
                jnp.full((1, TILE), MASKED, f32),
                jnp.zeros((1, TILE), f32),
                jnp.zeros((HEAD_DIM, TILE), f32),
            ),
        )
        att_ref[qt] = acc / total
        log_ref[qt] = high + jnp.log(total)
        return carry

    lax.fori_loop(0, n_q // per, one_query_tile, 0)
    head_scale = hs_ref[0]

    def load(u):
        return att_ref[u // per, :, (u % per) * 128 : (u % per) * 128 + 128]

    def give(t, tile):
        scaled_ref[t] = (tile * head_scale).astype(jnp.bfloat16)

    unsort_tiles(load, n_q, give)


def attend_back_kernel(
    info_ref, qs_ref, ks_ref, vs_ref, att_ref, log_ref, go_ref, dq_ref, dk_ref, dv_ref, dsum_ref,
    go_s, kn_ref, vn_ref, dq_s, dk_s, dv_s,
    *, n_q, n_k,
):
    per = TILE // 128
    f32 = jnp.float32
    low = jnp.bfloat16

    def store(u, tile):
        go_s[u // per, :, (u % per) * 128 : (u % per) * 128 + 128] = tile.astype(low)

    sort_tiles(lambda t: go_ref[t].astype(f32), n_q, store)
    for kt in range(n_k // per):
        kn_ref[kt] = ks_ref[kt].astype(f32).T.astype(low)
        vn_ref[kt] = vs_ref[kt].astype(f32).T.astype(low)
        dk_s[kt] = jnp.zeros((TILE, HEAD_DIM), f32)
        dv_s[kt] = jnp.zeros((TILE, HEAD_DIM), f32)
    dsum_ref[...] = jnp.zeros((1, TILE), f32)

    def one_query_tile(qt, carry):
        q_first, k_low = tile_spans(info_ref, qt, n_q // per, n_q * 64, 2 * n_k)
        q_pos, floor = query_rows(info_ref, q_first)
        q_t = qs_ref[qt]
        g_t = go_s[qt]
        q_n = q_t.astype(f32).T.astype(low)
        g_n = g_t.astype(f32).T.astype(low)
        log_total = log_ref[qt]
        delta = jnp.sum(g_t.astype(f32) * att_ref[qt], axis=0, keepdims=True)
        dsum_ref[...] += delta

        def one_key_tile(kt, acc):
            scores = dot(kn_ref[kt], q_t) * SCALE
            usable = usable_mask(q_pos, floor, kt)
            probs = jnp.where(usable, jnp.exp(scores - log_total), 0.0)
            grad_probs = dot(vn_ref[kt], g_t)
            grad_scores = (probs * (grad_probs - delta)).astype(low)
            dv_s[kt] += dot(probs.astype(low), g_n)
            dk_s[kt] += dot(grad_scores, q_n)
            return acc + dot(ks_ref[kt], grad_scores)

        dq_s[qt] = lax.fori_loop(
            k_low, q_first // TILE + 1, one_key_tile, jnp.zeros((HEAD_DIM, TILE), f32)
        )
        return carry

    lax.fori_loop(0, n_q // per, one_query_tile, 0)

    def load_q(u):
        return dq_s[u // per, :, (u % per) * 128 : (u % per) * 128 + 128]

    def give_q(t, tile):
        dq_ref[t] = (tile * SCALE).astype(dq_ref.dtype)

    def load_k(u):
        return dk_s[u // per, (u % per) * 128 : (u % per) * 128 + 128, :].T

    def give_k(t, tile):
        dk_ref[t] = (tile * SCALE).astype(dk_ref.dtype)

    def load_v(u):
        return dv_s[u // per, (u % per) * 128 : (u % per) * 128 + 128, :].T

    def give_v(t, tile):
        dv_ref[t] = tile.astype(dv_ref.dtype)

    unsort_tiles(load_q, n_q, give_q)
    unsort_tiles(load_k, n_k, give_k)
    unsort_tiles(load_v, n_k, give_v)


def head_grad_kernel(x_ref, dq_ref, dk_ref, dv_ref, m_ref, c_ref):
    low, f32 = jnp.bfloat16, jnp.float32

    @pl.when(pl.program_id(0) == 0)
    def _():
        m_ref[...] = jnp.zeros(m_ref.shape, f32)
        c_ref[...] = jnp.zeros(c_ref.shape, f32)

    x = jnp.concatenate([x_ref[0], x_ref[1]], axis=0).astype(f32)
    normed = normalize(x)[0].astype(low)
    grads = jnp.concatenate(
        [jnp.concatenate([ref[0], ref[1]], axis=1) for ref in (dq_ref, dk_ref, dv_ref)], axis=0
    )
    m_ref[...] += dot(grads, normed)
    c_ref[...] += dot(jnp.ones((8, grads.shape[1]), low), grads, 1, 1)


def takes(microseconds):
    return pl.CostEstimate(
        flops=0, transcendentals=0, bytes_accessed=int(microseconds * 3.2e6)
    )


def on_chip(n):
    return [pl.BlockSpec(memory_space=pltpu.VMEM)] * n


def in_scalars(n):
    return [pl.BlockSpec(memory_space=pltpu.SMEM)] * n


def attend(info, head_scale, q_tiles, kv_tiles, k_at):
    n_q, n_k = q_tiles.shape[0], kv_tiles.shape[0]
    nq, nk = n_q * 128 // TILE, n_k * 128 // TILE
    low, f32 = jnp.bfloat16, jnp.float32
    return pl.pallas_call(
        partial(attend_kernel, n_q=n_q, n_k=n_k, k_at=k_at),
        in_specs=in_scalars(2) + on_chip(2),
        out_specs=tuple(on_chip(6)),
        out_shape=(
            jax.ShapeDtypeStruct((n_q, HEAD_DIM, 128), low),
            jax.ShapeDtypeStruct((nq, HEAD_DIM, TILE), f32),
            jax.ShapeDtypeStruct((nq, 1, TILE), f32),
            jax.ShapeDtypeStruct((nq, HEAD_DIM, TILE), low),
            jax.ShapeDtypeStruct((nk, HEAD_DIM, TILE), low),
            jax.ShapeDtypeStruct((nk, HEAD_DIM, TILE), low),
        ),
        scratch_shapes=[pltpu.VMEM((nk, TILE, HEAD_DIM), low)],
        compiler_params=pltpu.CompilerParams(vmem_limit_bytes=48 << 20),
        cost_estimate=takes(10),
        name="attend",
    )(info, head_scale, q_tiles, kv_tiles)


def attend_back(info, qs, ks, vs, att, log_total, grad_tiles, kv_type):
    n_q = grad_tiles.shape[0]
    nq, nk = qs.shape[0], ks.shape[0]
    n_k = nk * TILE // 128
    low, f32 = jnp.bfloat16, jnp.float32
    return pl.pallas_call(
        partial(attend_back_kernel, n_q=n_q, n_k=n_k),
        in_specs=in_scalars(1) + on_chip(6),
        out_specs=tuple(on_chip(4)),
        out_shape=(
            jax.ShapeDtypeStruct((n_q, HEAD_DIM, 128), low),
            jax.ShapeDtypeStruct((n_k, HEAD_DIM, 128), kv_type),
            jax.ShapeDtypeStruct((n_k, HEAD_DIM, 128), kv_type),
            jax.ShapeDtypeStruct((1, TILE), f32),
        ),
        scratch_shapes=[
            pltpu.VMEM((nq, HEAD_DIM, TILE), low),
            pltpu.VMEM((nk, TILE, HEAD_DIM), low),
            pltpu.VMEM((nk, TILE, HEAD_DIM), low),
            pltpu.VMEM((nq, HEAD_DIM, TILE), f32),
            pltpu.VMEM((nk, TILE, HEAD_DIM), f32),
            pltpu.VMEM((nk, TILE, HEAD_DIM), f32),
        ],
        compiler_params=pltpu.CompilerParams(vmem_limit_bytes=48 << 20),
        cost_estimate=takes(10),
        name="attend_back",
    )(info, qs, ks, vs, att, log_total, grad_tiles)


def stream_tiles(gathered, which):
    _, _, rows, width = gathered.shape
    return pl.BlockSpec((2, pl.Squeezed(), rows, width), lambda i: (i, which, 0, 0))


def head_grad(gathered, dq, dk, dv):
    width = gathered.shape[3]
    f32 = jnp.float32
    tiles = pl.BlockSpec((2, HEAD_DIM, 128), lambda i: (i, 0, 0))
    return pl.pallas_call(
        head_grad_kernel,
        grid=(gathered.shape[0] // 2,),
        in_specs=[stream_tiles(gathered, 0)] + [tiles] * 3,
        out_specs=(
            pl.BlockSpec((3 * HEAD_DIM, width), lambda i: (0, 0)),
            pl.BlockSpec((8, 3 * HEAD_DIM), lambda i: (0, 0)),
        ),
        out_shape=(
            jax.ShapeDtypeStruct((3 * HEAD_DIM, width), f32),
            jax.ShapeDtypeStruct((8, 3 * HEAD_DIM), f32),
        ),
        cost_estimate=takes(8),
        name="head_grad",
    )(gathered, dq, dk, dv)


def place_sums_kernel(
    at_a_ref, at_b_ref, a_near_ref, a_far_ref, b_near_ref, b_far_ref, fc1_ref, out_ref
):
    f32 = jnp.float32
    per, n, hidden_width = fc1_ref.shape
    half = a_near_ref.shape[0]
    cut_at = a_near_ref.shape[2]
    rest = hidden_width - cut_at

    def put_a(i, ref, at):
        fc1_ref[i, :, :cut_at] = ref[at].astype(f32)

    def put_b(i, ref, at):
        fc1_ref[i, :, cut_at:] = ref[at, :, :rest].astype(f32)
        out_ref[i] = ref[at, :, rest:].astype(f32)

    for i in range(per):
        r = pl.program_id(0) * per + i
        for put, at, near, far in (
            (put_a, at_a_ref[r], a_near_ref, a_far_ref),
            (put_b, at_b_ref[r], b_near_ref, b_far_ref),
        ):
            pl.when(at < half)(partial(put, i, near, at))
            pl.when(at >= half)(partial(put, i, far, at - half))


def place_sums(at_a, at_b, sums_a, sums_b, hidden_width):
    half, n, wide_a = sums_a[0].shape
    wide_b = sums_b[0].shape[2]
    blocks = 2 * half
    per = 4
    width = wide_a + wide_b - hidden_width
    f32 = jnp.float32

    def out_block(w):
        return pl.BlockSpec((per, n, w), lambda r, at_a_ref, at_b_ref: (r, 0, 0))

    return pl.pallas_call(
        place_sums_kernel,
        grid_spec=pltpu.PrefetchScalarGridSpec(
            num_scalar_prefetch=2,
            grid=(blocks // per,),
            in_specs=on_chip(4),
            out_specs=(out_block(hidden_width), out_block(width)),
        ),
        out_shape=(
            jax.ShapeDtypeStruct((blocks, n, hidden_width), f32),
            jax.ShapeDtypeStruct((blocks, n, width), f32),
        ),
        compiler_params=pltpu.CompilerParams(vmem_limit_bytes=48 << 20),
        cost_estimate=takes(7),
        name="place_sums",
    )(at_a, at_b, *sums_a, *sums_b)


def place_qkv_kernel(
    at_l_ref, at_r_ref, left_ref, right_ref, weight_ref, gain_ref, bias_ref,
    grad_ref, gain_sum_ref, bias_sum_ref, scale_ref, small_ref,
):
    f32 = jnp.float32
    step = pl.program_id(0)
    n_rows = 3 * HEAD_DIM
    half = left_ref.shape[2]
    pairs = grad_ref.shape[1] // 128
    per = HEADS // 2 // pairs
    which = step // per
    row = lax.broadcasted_iota(jnp.int32, (16, 128), 0)
    lane = lax.broadcasted_iota(jnp.int32, (1, 128), 1)

    def extra_row(head, i):
        rows = left_ref[at_l_ref[head], n_rows : n_rows + 16, :128].astype(f32)
        return jnp.sum(jnp.where((row == i) | (row == i + 4), rows, 0.0), axis=0, keepdims=True)

    @pl.when(step == 0)
    def _():
        gain_sum_ref[...] = jnp.zeros(gain_sum_ref.shape, f32)
        bias_sum_ref[...] = jnp.zeros(bias_sum_ref.shape, f32)
        for side, ref in enumerate((left_ref, right_ref)):
            small_ref[:, side * half : side * half + half] = sum(
                ref[head, n_rows + 16 :, :].astype(f32) for head in range(HEADS)
            )
        for head in range(HEADS):
            scale_ref[head : head + 1, :] = extra_row(head, 3)

    rows = pl.ds(pl.multiple_of(which * HEAD_DIM, HEAD_DIM), HEAD_DIM)
    for pair in range(pairs):
        first = 2 * (step % per * pairs + pair)
        j = slice(pair * 128, pair * 128 + 128)
        columns = jnp.where(lane < HEAD_DIM, extra_row(first, which), extra_row(first + 1, which))
        for side, (ref, at_ref) in enumerate(((left_ref, at_l_ref), (right_ref, at_r_ref))):
            sums = jnp.concatenate(
                [ref[at_ref[first], rows, :], ref[at_ref[first + 1], rows, :]], axis=0
            ).astype(f32).T
            d = slice(side * half, side * half + half)
            weight = weight_ref[d, j].astype(f32)
            grad_ref[d, j] = sums * gain_ref[d, :] + bias_ref[d, :] * columns
            gain_sum_ref[d, :] += weight * sums
            bias_sum_ref[d, :] += weight * columns


def place_qkv(at_l, at_r, left, right, weight, gain, bias):
    wide, n_columns = weight.shape
    f32 = jnp.float32
    step = 512

    def whole(shape):
        return pl.BlockSpec(shape, lambda i, at_l_ref, at_r_ref: (0,) * len(shape))

    column = pl.BlockSpec((wide, step), lambda i, at_l_ref, at_r_ref: (0, i))
    outs = ((wide, 128), (wide, 128), (HEADS, 128), (16, wide))
    return pl.pallas_call(
        place_qkv_kernel,
        grid_spec=pltpu.PrefetchScalarGridSpec(
            num_scalar_prefetch=2,
            grid=(n_columns // step,),
            in_specs=[
                whole(left.shape), whole(right.shape), column, whole((wide, 1)), whole((wide, 1)),
            ],
            out_specs=(column,) + tuple(whole(shape) for shape in outs),
        ),
        out_shape=(jax.ShapeDtypeStruct((wide, n_columns), f32),)
        + tuple(jax.ShapeDtypeStruct(shape, f32) for shape in outs),
        compiler_params=pltpu.CompilerParams(vmem_limit_bytes=48 << 20),
        cost_estimate=takes(9),
        name="place_qkv",
    )(at_l, at_r, left, right, weight, gain[:, None], bias[:, None])


def from_member(value, s, size):
    return lax.ppermute(value, "fsdp", [((i + s) % size, i) for i in range(size)])


def gather_parts(shard, size):
    return [shard] + [from_member(shard, s, size) for s in range(1, size)]


def part_of(value, s, me, size, axis):
    width = value.shape[axis] // size
    return lax.dynamic_slice_in_dim(value, ((me + s) % size) * width, width, axis)


def natural(parts, me, axis):
    size = len(parts)
    twice = jnp.concatenate(parts + parts, axis=axis)
    width = parts[0].shape[axis]
    return lax.dynamic_slice_in_dim(twice, ((size - me) % size) * width, size * width, axis)


def times_parts(value, parts, me):
    size = len(parts)
    total = dot(part_of(value, 0, me, size, 1), parts[0])
    for s in range(1, size):
        total = total + dot(part_of(value, s, me, size, 1), parts[s])
    return total


def all_tokens(value, size):
    return jnp.concatenate([value] + [from_member(value, s, size) for s in range(1, size)], axis=0)


def all_tokens_own(value, me, size):
    pieces = [part_of(value, 0, me, size, 1)]
    for s in range(1, size):
        pieces.append(from_member(part_of(value, size - s, me, size, 1), s, size))
    return jnp.concatenate(pieces, axis=0)


def swapped(value, stride, groups):
    return lax.ppermute(value, "ctx", [(i, i ^ stride) for i in range(groups)])


def half_of(value, which, axis=0):
    n = value.shape[axis] // 2
    return lax.dynamic_slice_in_dim(value, which * n, n, axis)


def bit_of(member, stride):
    return (member // stride) % 2


def from_line(value, k, plane, groups):
    return lax.ppermute(value, "ctx", [(i, (i + k * plane) % groups) for i in range(groups)])


def joined_places(lines_of, bits_of, order, member, line, lines, plane):
    place = (line - lines_of) % lines
    step = lines
    for i in order:
        place = place + (bits_of[i] ^ bit_of(member, 1 << i)) * step
        step = 2 * step
    return place.astype(jnp.int32)


def local(
    inputs, cotangent, doc_lengths, qkv_weight, out_weight, fc1_weight, fc2_weight,
    norm_gain, norm_bias, mid_gain, mid_bias, head_scale,
):
    low, f32 = jnp.bfloat16, jnp.float32
    groups = lax.axis_size("ctx")
    size = lax.axis_size("fsdp")
    member = lax.axis_index("ctx")
    me = lax.axis_index("fsdp")
    x_low = inputs[0]
    rows, width = x_low.shape
    hidden_width = fc1_weight.shape[1]
    copies = groups // HEADS
    head_groups = [[g * HEADS + i for i in range(HEADS)] for g in range(copies)]
    copy_groups = [[g * HEADS + i for g in range(copies)] for i in range(HEADS)]
    head = member % HEADS
    lines = 1
    while lines * lines < groups:
        lines = 2 * lines
    plane = groups // lines
    line = member // plane
    strides = [1 << i for i in range(plane.bit_length() - 1)]
    info = jnp.concatenate([(member // HEADS)[None].astype(jnp.int32), doc_lengths[0]])

    gathered = lax.all_gather(
        x_low[None],
        "ctx", axis=0, axis_index_groups=None if copies == 1 else head_groups,
    )
    norm_vecs = jnp.concatenate([norm_gain, norm_bias], axis=0)
    norm_vecs = natural(gather_parts(norm_vecs, size), me, 1).astype(f32)
    norm_vecs, qkv_shard = lax.optimization_barrier((norm_vecs, qkv_weight))
    gains, biases = norm_vecs[:3], norm_vecs[3:]
    qkv_parts = gather_parts(qkv_shard, size)

    x_local = x_low.astype(f32)
    norm_one, inv_one = normalize(x_local)
    normed_one = (norm_one * gains[0] + biases[0]).astype(low)
    normed_one, small, out_shard, fc1_shard, fc2_shard = lax.optimization_barrier(
        (
            normed_one, jnp.concatenate([mid_gain, mid_bias, head_scale]),
            out_weight, fc1_weight, fc2_weight,
        )
    )
    smalls = gather_parts(small, size)
    out_parts = gather_parts(out_shard, size)
    fc1_parts = gather_parts(fc1_shard, size)
    fc2_parts = gather_parts(fc2_shard, size)
    n_mid = mid_gain.size
    cut = [0, n_mid, 2 * n_mid, small.size]
    mid_gains, mid_biases, head_scales = (
        natural([v[cut[i] : cut[i + 1]] for v in smalls], me, 0).astype(f32) for i in range(3)
    )
    my_scale = lax.dynamic_slice_in_dim(head_scales, head, 1, 0)
    project_t = sum(
        dot(qkv_parts[s], part_of(normed_one, s, me, size, 1), 0, 1) for s in range(size)
    ).astype(low)
    by_head = project_t.reshape(3, HEADS, HEAD_DIM, rows).transpose(1, 0, 2, 3)
    qkv_tiles = lax.all_to_all(by_head, "ctx", 0, 0, tiled=True, axis_index_groups=head_groups)
    if copies == 1:
        kv_tiles, k_at = qkv_tiles, 1
    else:
        kv_tiles, k_at = lax.all_gather(
            qkv_tiles[:, 1:], "ctx", axis=0, tiled=True, axis_index_groups=copy_groups
        ), 0
    scaled_tiles, att, log_total, qs, ks, vs = attend(info, my_scale, qkv_tiles, kv_tiles, k_at)
    scaled_t = lax.all_to_all(
        scaled_tiles, "ctx", 0, 0, tiled=True, axis_index_groups=head_groups
    ).reshape(width, rows)
    branch = sum(dot(part_of(scaled_t, s, me, size, 0), out_parts[s], 0, 0) for s in range(size))
    norm_att, inv_att = normalize(branch)
    attn_out = norm_att * gains[1] + biases[1]
    middle = x_local + attn_out
    norm_two, inv_two = normalize(middle)
    normed_two = (norm_two * gains[2] + biases[2]).astype(low)
    hidden = times_parts(normed_two, fc1_parts, me)
    active, gelu_back = jax.vjp(partial(jax.nn.gelu, approximate=True), hidden)
    norm_mid, inv_mid = normalize(active)
    mixed_in = (norm_mid * mid_gains + mid_biases).astype(low)
    ffn_out = times_parts(mixed_in, fc2_parts, me)
    result = middle + ffn_out

    grad_ffn = cotangent[0]
    grad_top = grad_ffn.astype(f32)
    fc2_grad = dot(
        all_tokens_own(mixed_in, me, size), all_tokens(grad_ffn, size), 0, 0
    ).astype(low)
    fc2_grad, norm_mid = lax.optimization_barrier((fc2_grad, norm_mid))
    fc2_sum = lax.psum(fc2_grad, "ctx")
    grad_mixed = natural([dot(grad_ffn, part, 1, 1) for part in fc2_parts], me, 1)
    grad_active, mid_gain_grad, mid_bias_grad = norm_backward(
        grad_mixed, norm_mid, inv_mid, mid_gains
    )
    grad_hidden = gelu_back(grad_active)[0].astype(low)
    fc1_left = all_tokens_own(normed_two, me, size)
    fc1_right = all_tokens(grad_hidden, size)
    grad_two = natural([dot(grad_hidden, part, 1, 1) for part in fc1_parts], me, 1)
    grad_mid_in, gain_two, bias_two = norm_backward(grad_two, norm_two, inv_two, gains[2])
    grad_middle = grad_top + grad_mid_in
    grad_branch_f, gain_att, bias_att = norm_backward(grad_middle, norm_att, inv_att, gains[1])
    grad_branch = grad_branch_f.astype(low)
    out_left = all_tokens_own(scaled_t.T, me, size)
    out_right = all_tokens(grad_branch, size)

    wide = norm_gain.shape[1]
    squares = jnp.stack(
        [jnp.sum(result * result), jnp.sum(attn_out * attn_out), jnp.sum(ffn_out * ffn_out)]
    )
    norms = jnp.stack([gain_att, gain_two, bias_att, bias_two])
    mids = jnp.stack([mid_gain_grad, mid_bias_grad])
    n_small = 4 + 2 * mid_gain.shape[0] // wide

    def small_rows(s):
        return jnp.concatenate(
            [
                part_of(norms, s, me, size, 1),
                part_of(mids, s, me, size, 1).reshape(-1, wide),
                jnp.pad(squares[None], ((0, 15 - n_small), (0, wide - 3))),
            ],
            axis=0,
        )

    own_rows = fc1_weight.shape[0]

    cut_at = (hidden_width + width) // 2

    def product_a(w):
        return dot(half_of(fc1_left, w, 1), fc1_right[:, :cut_at], 0, 0)

    def product_b(w):
        return jnp.concatenate(
            [
                dot(half_of(fc1_left, w, 1), fc1_right[:, cut_at:], 0, 0),
                dot(half_of(out_left, w, 1), out_right, 0, 0),
            ],
            axis=1,
        )

    sent_a = product_a(1 - bit_of(member, strides[0])).astype(low)
    sent_b = product_b(1 - bit_of(member, strides[-1])).astype(low)

    grad_scaled_t = natural([dot(part, grad_branch, 1, 1) for part in out_parts], me, 0)
    grad_att = (
        grad_scaled_t.reshape(HEADS, HEAD_DIM, rows) * head_scales[:, None, None]
    ).astype(low)
    grad_tiles = lax.all_to_all(grad_att, "ctx", 0, 0, tiled=True, axis_index_groups=head_groups)
    grad_tiles, sent_a, sent_b = lax.optimization_barrier((grad_tiles, sent_a, sent_b))
    orders = (strides, strides[::-1])
    got = [swapped(v, o[0], groups) for v, o in zip((sent_a, sent_b), orders)]
    dq, dk, dv, delta_sum = attend_back(
        info, qs, ks, vs, att, log_total, grad_tiles, low if copies == 1 else f32
    )
    if copies > 1:
        dk, dv = (
            lax.psum_scatter(
                d, "ctx", scatter_dimension=0, tiled=True, axis_index_groups=copy_groups
            ).astype(low)
            for d in (dk, dv)
        )

    grads_out = jnp.stack([dq, dk, dv], axis=1)
    grad_proj_t = lax.all_to_all(
        grads_out, "ctx", 0, 0, tiled=True, axis_index_groups=head_groups
    ).transpose(1, 0, 2, 3).reshape(3 * width, rows)
    head_sums, column_sums = head_grad(gathered, dq, dk, dv)
    my_scale_grad = jnp.sum(delta_sum) / my_scale[0]
    extra = jnp.concatenate(
        [column_sums[0].reshape(3, HEAD_DIM), jnp.full((1, HEAD_DIM), my_scale_grad)], axis=0
    )
    smalls_of = [small_rows(s) for s in range(size)]
    if copies > 1:
        head_sums, extra, smalls_of = (
            lax.psum(d, "ctx", axis_index_groups=copy_groups)
            for d in (head_sums, extra, smalls_of)
        )
    n_head_rows = head_sums.shape[0]
    n_payload = n_head_rows + 32
    extra = jnp.pad(jnp.concatenate([extra, extra], axis=1), ((0, 12), (0, wide - 2 * HEAD_DIM)))

    def with_extra(sums, more, small_sums):
        high = more.astype(low)
        rest_of = (more - high.astype(f32)).astype(low)
        both_parts = high + jnp.roll(rest_of, 4, axis=0)
        return jnp.concatenate([sums.astype(low), both_parts, small_sums.astype(low)], axis=0)

    own_sums = part_of(head_sums, 0, me, size, 1)
    own_extra = extra
    own_small = smalls_of[0]
    for s in range(1, size):
        more_rows = from_member(
            with_extra(part_of(head_sums, size - s, me, size, 1), extra, smalls_of[size - s]),
            s, size,
        ).astype(f32)
        own_sums = own_sums + more_rows[:n_head_rows]
        own_small = own_small + more_rows[n_head_rows + 16 :]
        more_rows = more_rows[n_head_rows : n_head_rows + 16]
        own_extra = own_extra + jnp.pad(more_rows[:4] + more_rows[4:8], ((0, 12), (0, 0)))
    payload = lax.optimization_barrier(with_extra(own_sums, own_extra, own_small))

    got, payload = lax.optimization_barrier((got, payload))
    sums = [
        (product(bit_of(member, o[0])) + g.astype(f32)).astype(low)
        for product, o, g in zip((product_a, product_b), orders, got)
    ]
    for step in range(1, len(strides)):
        bits_now = [bit_of(member, o[step]) for o in orders]
        got = [
            swapped(half_of(v, 1 - bit), o[step], groups)
            for v, bit, o in zip(sums, bits_now, orders)
        ]
        sums = [
            (half_of(v, bit).astype(f32) + g.astype(f32)).astype(low)
            for v, bit, g in zip(sums, bits_now, got)
        ]
    unit = jnp.concatenate(sums, axis=1)
    one_chunk = own_rows // groups
    sent = [
        lax.dynamic_slice_in_dim(unit, (line + k) % lines * one_chunk, one_chunk, 0)
        for k in range(lines)
    ]
    on_lines = [from_line(sent[k], k, plane, groups) for k in range(1, lines)]
    by_permutes = copies == 1
    unit = (sent[0].astype(f32) + sum(g.astype(f32) for g in on_lines)).astype(low)
    got = [from_line(unit, k, plane, groups) for k in range(1, lines)]
    on_line = [payload]
    if by_permutes:
        on_line += [from_line(payload, k, plane, groups) for k in range(1, lines)]
    got, on_line = lax.optimization_barrier((got, on_line))
    near = []
    if by_permutes:
        on_line = jnp.concatenate(on_line, axis=0)
        near = [on_line[:, : wide // 2], on_line[:, wide // 2 :]]
        near = [[v, swapped(v, o[0], groups)] for v, o in zip(near, orders)]
    unit = jnp.concatenate([unit] + got, axis=0)
    parts = [unit[:, :cut_at], unit[:, cut_at:]]
    outward = orders[::-1]
    for step in range(len(strides) - 1):
        got = [swapped(v, o[step], groups) for v, o in zip(parts, outward)]
        got, near = lax.optimization_barrier((got, near))
        parts = [jnp.concatenate([v, g], axis=0) for v, g in zip(parts, got)]
    if by_permutes:
        near = [jnp.concatenate(v, axis=0) for v in near]
        near = [[v, swapped(v, o[1], groups)] for v, o in zip(near, orders)]
    far = [swapped(v, o[-1], groups) for v, o in zip(parts, outward)]

    bits = range(len(strides))
    heads = jnp.arange(HEADS)
    if by_permutes:
        left, right = (
            jnp.concatenate(v, axis=0).reshape(HEADS, n_payload, wide // 2) for v in near
        )
        head_bits = [bit_of(heads, stride) for stride in strides]
        at_l = joined_places(heads // plane, head_bits, bits, member, line, lines, plane)
        at_r = joined_places(heads // plane, head_bits, bits[::-1], member, line, lines, plane)
    else:
        every = lax.all_gather(payload, "ctx", axis=0, axis_index_groups=head_groups)
        left, right = every[:, :, : wide // 2], every[:, :, wide // 2 :]
        at_l = at_r = heads.astype(jnp.int32)
    qkv_sum, gain_parts, bias_parts, scales, small_sums = place_qkv(
        at_l, at_r, left, right, qkv_weight, norm_gain[0].astype(f32), norm_bias[0].astype(f32)
    )
    gain_one, bias_one = jnp.sum(gain_parts, axis=1), jnp.sum(bias_parts, axis=1)
    scale_sum = part_of(scales[:, 0], 0, me, size, 0)
    grad_one = natural([dot(grad_proj_t, part, 0, 1) for part in qkv_parts], me, 1)
    grad_first = norm_backward(grad_one, norm_one, inv_one, gains[0])[0]
    input_grad = (grad_middle + grad_first).astype(low)[None]

    fc2_sum, qkv_sum = lax.optimization_barrier((fc2_sum, qkv_sum))
    fc2_sum = fc2_sum.astype(f32)
    far, fc2_sum = lax.optimization_barrier((far, fc2_sum))
    far, qkv_sum, input_grad = lax.optimization_barrier((far, qkv_sum, input_grad))
    block = jnp.arange(groups)
    block_bits = [block // lines // (1 << i) % 2 for i in bits]
    at_a = joined_places(
        block % lines, block_bits[::-1], bits[::-1], member, line, lines, plane
    )
    at_b = joined_places(block % lines, block_bits, bits, member, line, lines, plane)
    ends = [
        [d.reshape(groups // 2, one_chunk, -1) for d in pair] for pair in zip(parts, far)
    ]
    fc1_sum, out_sum = place_sums(at_a, at_b, ends[0], ends[1], hidden_width)
    fc1_sum = fc1_sum.reshape(own_rows, hidden_width)
    out_sum = out_sum.reshape(own_rows, width)
    gain_grad = jnp.stack([gain_one, small_sums[0], small_sums[1]])
    bias_grad = jnp.stack([bias_one, small_sums[2], small_sums[3]])
    mid_sums = small_sums[4:n_small].reshape(2, -1)
    mid_gain_sum, mid_bias_sum = mid_sums[0], mid_sums[1]
    rms_values = jnp.sqrt(small_sums[n_small, :3] / (rows * groups * size * width))
    return (
        result.astype(low)[None],
        input_grad,
        qkv_sum,
        out_sum,
        fc1_sum,
        fc2_sum,
        gain_grad,
        bias_grad,
        mid_gain_sum,
        mid_bias_sum,
        scale_sum,
        rms_values,
    )


def solution(mesh):
    split = P("fsdp", "ctx", None)
    by_row = P("fsdp", None)
    by_col = P(None, "fsdp")
    one = P("fsdp")
    return jax.shard_map(
        local,
        mesh=mesh,
        in_specs=(split, split, by_row, by_row, by_row, by_row, by_row, by_col, by_col, one, one, one),
        out_specs=(split, split, by_row, by_row, by_row, by_row, by_col, by_col, one, one, one, P()),
        check_vma=False,
    )
```
